512 devices in a mesh: plane: 8 (over x, core), span: 16 (over z), height: 4 (over y).
Axes of the slice: x: 4, y: 4, z: 16, core: 2. Of those that a mesh axis runs over, the one named last changes fastest.
Arguments:
- noisy: bfloat16 [8, 3, 256, 2048], P('plane', None, 'height', 'span'), may hold values from -6 to 6
- coarse_cond: bfloat16 [512, 8, 3, 32, 256], P(('plane', 'span', 'height')), may hold values from -6 to 6
- timestep: int32 [1], replicated, may hold values from 20 to 899
- owner: int32 [1], replicated, may hold values from 0 to 511
- w_embed: float32 [64, 256], replicated, may hold values from -0.75 to 0.75
- w_biases: float32 [256, 448], replicated, may hold values from -0.375 to 0.375
- w_enter: bfloat16 [3, 64, 18], replicated, may hold values from -1.5 to 1.5
- pool_fine: bfloat16 [4, 128, 64], replicated, may hold values from -0.5 to 0.5
- pool_mid: bfloat16 [4, 256, 128], replicated, may hold values from -0.375 to 0.375
- w_squeeze: bfloat16 [128, 256], replicated, may hold values from -0.375 to 0.375
- w_across: bfloat16 [3, 256, 128], replicated, may hold values from -0.5 to 0.5
- w_middle: bfloat16 [3, 256, 768], replicated, may hold values from -0.21875 to 0.21875
- rise_mid: bfloat16 [4, 128, 256], replicated, may hold values from -0.5 to 0.5
- decode_mid: bfloat16 [3, 128, 384], replicated, may hold values from -0.3125 to 0.3125
- rise_fine: bfloat16 [4, 64, 128], replicated, may hold values from -0.75 to 0.75
- decode_fine: bfloat16 [3, 64, 192], replicated, may hold values from -0.4375 to 0.4375
- w_leave: bfloat16 [3, 3, 192], replicated, may hold values from -0.4375 to 0.4375
Outputs:
- noise_pred: bfloat16 [8, 3, 256, 2048], P('plane', None, 'height', 'span')
- next_sample: float32 [8, 3, 256, 2048], P('plane', None, 'height', 'span')
The draws below stay inside these ranges and needn't reach their ends.
Inputs may be any that keep to these rules, and one draw needn't show every extreme that they name: The timestep lies in the plan's range and is at least 20. The owner is a device index in the mesh order plane, span, height.
All inputs are finite; a program needn't handle non-finite values.
Results may differ from the reference program's by a relative error of at most 0.03.
Values may be sent and summed in bfloat16 or wider, within the bound.
A program may use at most 64 MiB of HBM per device.

```python
import math
import jax
import jax.numpy as jnp
from jax import lax

CH1 = 64
CH2 = 128
CH3 = 256
INNER = 128
TSIN = 64
TEMB = 256
CF = 8
TSTEPS = 1000
STRIDE = 20
NP = 8
HEIGHT = 256
SPAN = 2048
CHC = 32
CSC = 256
DEVICES = 512


def level_of(rng, shape, split, smallest, high):
    def one(dim, parts):
        heights = jax.random.uniform(jax.random.fold_in(jax.random.fold_in(rng, 6), dim), (parts,), jnp.float32, smallest / len(split), high / len(split))
        return jnp.repeat(jnp.exp(heights), shape[dim] // parts).reshape((-1,) + (1,) * (len(shape) - dim - 1))

    factor_of = one(*split[0])
    for cut in split[1:]:
        factor_of = factor_of * one(*cut)
    return factor_of


def centred(own_key, extent, scale, limit, split=(), kind=jnp.bfloat16):
    entries = scale * jax.random.normal(own_key, extent, jnp.float32)
    if split:
        entries = entries * level_of(own_key, extent, split, -0.22, 0.18)
    return jnp.clip(entries, -limit, limit).astype(kind)


def setup_inputs(seed: int = 0) -> dict:
    key_list = jax.random.split(jax.random.key(seed), 18)
    noisy = centred(key_list[0], (NP, 3, HEIGHT, SPAN), 1.0, 6.0, ((0, 8), (2, 4), (3, 16)))
    coarse_cond = centred(key_list[1], (DEVICES, NP, 3, CHC, CSC), 1.0, 6.0, ((0, 512),))
    timestep = jax.random.randint(key_list[2], (1,), STRIDE, 900).astype(jnp.int32)
    owner = jax.random.randint(key_list[3], (1,), 0, DEVICES).astype(jnp.int32)
    w_embed = centred(key_list[4], (TSIN, TEMB), TSIN ** -0.5, 0.75, (), jnp.float32)
    w_biases = centred(key_list[5], (TEMB, CH1 + CH2 + CH3), TEMB ** -0.5, 0.375, (), jnp.float32)
    w_enter = centred(key_list[6], (3, CH1, 18), 18 ** -0.5, 1.5)
    pool_fine = centred(key_list[7], (4, CH2, CH1), (2 * CH1) ** -0.5, 0.5)
    pool_mid = centred(key_list[8], (4, CH3, CH2), (2 * CH2) ** -0.5, 0.375)
    w_squeeze = centred(key_list[9], (INNER, CH3), CH3 ** -0.5, 0.375)
    w_across = centred(key_list[10], (3, CH3, INNER), INNER ** -0.5, 0.5)
    w_middle = centred(key_list[11], (3, CH3, 3 * CH3), (3 * CH3) ** -0.5, 0.21875)
    rise_mid = centred(key_list[12], (4, CH2, CH3), (CH3 // 2) ** -0.5, 0.5)
    decode_mid = centred(key_list[13], (3, CH2, 3 * CH2), (3 * CH2) ** -0.5, 0.3125)
    rise_fine = centred(key_list[14], (4, CH1, CH2), (CH2 // 2) ** -0.5, 0.75)
    decode_fine = centred(key_list[15], (3, CH1, 3 * CH1), (3 * CH1) ** -0.5, 0.4375)
    w_leave = centred(key_list[16], (3, 3, 3 * CH1), (3 * CH1) ** -0.5, 0.4375)
    return {"noisy": noisy, "coarse_cond": coarse_cond, "timestep": timestep, "owner": owner, "w_embed": w_embed, "w_biases": w_biases, "w_enter": w_enter, "pool_fine": pool_fine, "pool_mid": pool_mid, "w_squeeze": w_squeeze, "w_across": w_across, "w_middle": w_middle, "rise_mid": rise_mid, "decode_mid": decode_mid, "rise_fine": rise_fine, "decode_fine": decode_fine, "w_leave": w_leave}


def stencil(padded, weight, rows, cols):
    total = None
    for lift in range(3):
        stacked = jnp.concatenate([padded[:, lift:lift + rows, step:step + cols] for step in range(3)], axis=0)
        term = jnp.einsum('ok,khs->ohs', weight[lift].astype(jnp.float32), stacked.astype(jnp.float32), precision=lax.Precision.HIGHEST)
        total = term if total is None else total + term
    return total

def framed(field):
    return jnp.pad(field, ((0, 0), (1, 1), (1, 1)))

def pooled(field, weight):
    chans, rows, cols = field.shape
    outs = weight.shape[1]
    grid = field.reshape(chans, rows // 2, 2, cols // 2, 2).astype(jnp.float32)
    kernel = weight.reshape(2, 2, outs, chans).astype(jnp.float32)
    return jnp.einsum('aboc,cxayb->oxy', kernel, grid, precision=lax.Precision.HIGHEST)

def raised(field, weight):
    chans, rows, cols = field.shape
    outs = weight.shape[1]
    kernel = weight.reshape(2, 2, outs, chans).astype(jnp.float32)
    spread = jnp.einsum('aboc,cxy->oxayb', kernel, field.astype(jnp.float32), precision=lax.Precision.HIGHEST)
    return spread.reshape(outs, 2 * rows, 2 * cols)

def plan(stepnum):
    phase = (stepnum.astype(jnp.float32) / TSTEPS + 0.008) / 1.008 * (math.pi / 2.0)
    return jnp.cos(phase) ** 2

def time_bias(timestep, w_embed, w_biases):
    half = w_embed.shape[0] // 2
    freqs = jnp.exp(-math.log(10000.0) * jnp.arange(half, dtype=jnp.float32) / half)
    angles = timestep[0].astype(jnp.float32) * freqs
    waves = jnp.concatenate([jnp.sin(angles), jnp.cos(angles)])
    hidden = jax.nn.silu(jnp.dot(waves, w_embed, precision=lax.Precision.HIGHEST))
    return jnp.dot(hidden, w_biases, precision=lax.Precision.HIGHEST)

def reference(noisy, coarse_cond, timestep, owner, w_embed, w_biases, w_enter, pool_fine, pool_mid, w_squeeze, w_across, w_middle, rise_mid, decode_mid, rise_fine, decode_fine, w_leave):
    biases = time_bias(timestep, w_embed, w_biases)
    first = w_enter.shape[1]
    second = pool_fine.shape[1]
    bias_one = biases[:first][:, None, None]
    bias_two = biases[first:first + second][:, None, None]
    bias_three = biases[first + second:][:, None, None]
    cond = lax.dynamic_index_in_dim(coarse_cond, owner[0].astype(jnp.int32), 0, keepdims=False)
    lifted = jnp.repeat(jnp.repeat(cond, CF, axis=2), CF, axis=3)

    def encode(pair):
        sample, lift = pair
        rows, cols = (sample.shape[1], sample.shape[2])
        entry = jnp.concatenate([sample, lift], axis=0)
        level_one = jax.nn.silu(stencil(framed(entry), w_enter, rows, cols) + bias_one).astype(jnp.bfloat16)
        level_two = jax.nn.silu(pooled(level_one, pool_fine) + bias_two).astype(jnp.bfloat16)
        level_three = jax.nn.silu(pooled(level_two, pool_mid) + bias_three).astype(jnp.bfloat16)
        return (level_one, level_two, level_three)
    deepest = lax.map(lambda pair: encode(pair)[2], (noisy, lifted))
    squeezed = jnp.einsum('ic,pchs->pihs', w_squeeze.astype(jnp.float32), deepest.astype(jnp.float32), precision=lax.Precision.HIGHEST).astype(jnp.bfloat16)
    planes = noisy.shape[0]
    beside_all = jnp.pad(squeezed, ((1, 1), (0, 0), (0, 0), (0, 0)))
    mixed = deepest.astype(jnp.float32)
    for tap in range(3):
        mixed = mixed + jnp.einsum('oi,pihs->pohs', w_across[tap].astype(jnp.float32), beside_all[tap:tap + planes].astype(jnp.float32), precision=lax.Precision.HIGHEST)
    mixed = mixed.astype(jnp.bfloat16)

    def decode(triple):
        sample, lift, middle = triple
        level_one, level_two, unused = encode((sample, lift))
        rows, cols = (sample.shape[1], sample.shape[2])
        coarse = jax.nn.silu(stencil(framed(middle), w_middle, rows // 4, cols // 4)).astype(jnp.bfloat16)
        joined_two = (raised(coarse, rise_mid) + level_two.astype(jnp.float32)).astype(jnp.bfloat16)
        decoded_two = jax.nn.silu(stencil(framed(joined_two), decode_mid, rows // 2, cols // 2)).astype(jnp.bfloat16)
        joined_one = (raised(decoded_two, rise_fine) + level_one.astype(jnp.float32)).astype(jnp.bfloat16)
        decoded_one = jax.nn.silu(stencil(framed(joined_one), decode_fine, rows, cols)).astype(jnp.bfloat16)
        return stencil(framed(decoded_one), w_leave, rows, cols).astype(jnp.bfloat16)
    noise_pred = lax.map(decode, (noisy, lifted, mixed))
    now = plan(timestep[0])
    prior = plan(timestep[0] - STRIDE)
    sample_f = noisy.astype(jnp.float32)
    guess = noise_pred.astype(jnp.float32)
    clean = (sample_f - jnp.sqrt(1.0 - now) * guess) / jnp.sqrt(now)
    next_sample = jnp.sqrt(prior) * clean + jnp.sqrt(1.0 - prior) * guess
    return (noise_pred, next_sample)
```

```python
import math

import jax
import jax.numpy as jnp
from jax import lax
from jax.experimental import pallas as pl
from jax.experimental.pallas import tpu as pltpu
from jax.sharding import PartitionSpec as P

TSTEPS = 1000
STRIDE = 20
F32 = jnp.float32
BF16 = jnp.bfloat16
MESH = pl.DeviceIdType.MESH
HIGHEST = lax.Precision.HIGHEST


def nt(a, b):
    return lax.dot_general(a, b, (((1,), (1,)), ((), ())), preferred_element_type=F32)


def nn(a, b):
    return lax.dot_general(a, b, (((1,), (0,)), ((), ())), preferred_element_type=F32)


def silu(v):
    return v * (0.5 * jnp.tanh(0.5 * v) + 0.5)


def iota(shape, dim):
    return lax.broadcasted_iota(jnp.int32, shape, dim)


def onehot(cond):
    return jnp.where(cond, 1.0, 0.0).astype(BF16)


def roll_rows(v, shift):
    return pltpu.roll(v.astype(F32), shift, v.ndim - 2).astype(BF16)


def plan_of(step):
    phase = (step / TSTEPS + 0.008) / 1.008 * (math.pi / 2.0)
    return jnp.cos(phase) ** 2


WINDOW = ((0, 128), (256, 512), (384, 640), (768, 896))


def phase_window(main, side, x):
    def flat(v):
        return v.reshape(288, v.shape[-1])

    return jnp.concatenate(
        [
            flat(main[x, :, :, :, 128:256]),
            flat(side[x, 1:10, :, :, 128:256]),
            flat(main[x + 1]),
            flat(side[x + 1, 1:10]),
            flat(main[x + 2, :, :, :, 0:128]),
            flat(side[x + 2, 1:10, :, :, 0:128]),
        ],
        axis=1,
    )


def put_phases(main, side, rows, b, v):
    main[rows, :, b] = v
    below, above = (slice(1, 10), slice(2, 11)) if b else (slice(0, 9), slice(1, 10))
    for low in (0, 128):
        side[rows, below, 1 - b, :, low : low + 64] = v[..., low : low + 64]
        side[rows, above, 1 - b, :, low + 64 : low + 128] = v[..., low + 64 : low + 128]


def close_phases(main, side):
    right = roll_rows(main[1:11, 8, 1], 1)
    left = roll_rows(main[1:11, 0, 0], 15)
    for low in (0, 128):
        side[1:11, 1, 0, :, low + 64 : low + 128] = right[..., low + 64 : low + 128]
        side[1:11, 9, 1, :, low : low + 64] = left[..., low : low + 64]
    main[0, :, :, :, 128:256] = roll_rows(main[10, :, :, :, 128:256], 4)
    side[0, 1:10, :, :, 128:256] = roll_rows(side[10, 1:10, :, :, 128:256], 4)
    main[11, :, :, :, 0:128] = roll_rows(main[1, :, :, :, 0:128], 12)
    side[11, 1:10, :, :, 0:128] = roll_rows(side[1, 1:10, :, :, 0:128], 12)


def body(
    sizes,
    noisy,
    slot,
    timestep,
    owner,
    w_embed,
    w_biases,
    w_enter,
    pool_fine,
    pool_mid,
    w_squeeze,
    w_across,
    w_middle,
    rise_mid,
    decode_mid,
    rise_fine,
    decode_fine,
    w_leave,
    noise_out,
    next_out,
    send_p,
    got_p,
    planef,
    heightf,
    send_h,
    got_h,
    rowsf,
    send_s,
    got_s,
    around,
    aroundf,
    entryf,
    tapf,
    tap,
    condf,
    bias,
    w_in,
    w_pf,
    w_pm,
    w_ac,
    w_dm,
    w_df,
    leavef,
    w_lv,
    mask,
    h1,
    d1,
    d2,
    sq,
    mx,
    c3,
    v2,
    f1m,
    f1s,
    f2m,
    f2s,
    acc,
    turned,
    outf,
    guess,
    sem_p,
    sem_h,
    sem_s,
    sem_n,
    sem_x,
):
    planes, spans, heights = sizes
    p, s, h = (lax.axis_index(a) for a in ("plane", "span", "height"))

    def at(dp, ds, dh):
        return (
            lax.rem(p + (dp + planes), planes),
            lax.rem(s + (ds + spans), spans),
            lax.rem(h + (dh + heights), heights),
        )

    barrier = pltpu.get_barrier_semaphore()
    partners = [(k, 0, 0) for k in range(1, planes)]
    partners += [(0, k, 0) for k in range(1, spans)]
    partners += [(0, 0, k) for k in range(1, heights)]
    partners += [(0, ds, dh) for ds in (-1, 1) for dh in (-1, 1)]
    for offset in partners:
        pl.semaphore_signal(barrier, inc=1, device_id=at(*offset), device_id_type=MESH)
    pl.semaphore_wait(barrier, len(partners))

    def remote(src, dst, sems, index, offset):
        return pltpu.make_async_remote_copy(
            src_ref=src,
            dst_ref=dst,
            send_sem=sems.at[(0,) + index],
            recv_sem=sems.at[(1,) + index],
            device_id=at(*offset),
            device_id_type=MESH,
        )

    mine = (owner[0] == (p * spans + s) * heights + h).astype(F32)
    for k in range(planes):
        send_p[k] = (slot[0, k].astype(F32) * mine).astype(BF16)

    def copy_p(k):
        return remote(send_p.at[lax.rem(p + k, planes)], got_p.at[p], sem_p, (k,), (k, 0, 0))

    for k in range(1, planes):
        copy_p(k).start()
    got_p[p] = send_p[p]

    halo = []
    for ds in (-1, 0, 1):
        for dh in (-1, 0, 1):
            if ds == 0 and dh == 0:
                continue
            src = {-1: slice(0, 16), 0: slice(0, 64), 1: slice(48, 64)}[dh]
            dst = {-1: slice(80, 96), 0: slice(16, 80), 1: slice(0, 16)}[dh]
            halo.append(
                remote(
                    noisy.at[0, :, src], around.at[1 - ds, :, dst], sem_n, (len(halo),), (0, ds, dh)
                )
            )
    for copy in halo:
        copy.start()

    now_step = jnp.full((8, 128), timestep[0].astype(F32), F32)
    lane = iota((8, 64), 1)
    order = jnp.where(lane < 32, lane, lane - 32).astype(F32)
    angle = timestep[0].astype(F32) * jnp.exp(order * (-math.log(10000.0) / 32))
    waves = jnp.where(lane < 32, jnp.sin(angle), jnp.cos(angle))
    hidden = jnp.dot(waves, w_embed[...], precision=HIGHEST, preferred_element_type=F32)
    hidden = hidden / (1.0 + jnp.exp(-hidden))
    flat = jnp.dot(hidden, w_biases[...], precision=HIGHEST, preferred_element_type=F32)
    col = iota((448, 640), 1)
    pick = jnp.where(col < 256, lax.rem(col, 64), col - 192)
    pick = jnp.where(iota((448, 640), 0) == pick, 1.0, 0.0)
    bias[...] = jnp.dot(flat, pick, precision=HIGHEST, preferred_element_type=F32)

    w_df[...] = jnp.zeros_like(w_df)
    w_lv[...] = jnp.zeros_like(w_lv)
    leavef[...] = jnp.zeros_like(leavef)
    for b in (0, 1):
        place = iota((192, 256), 1)
        tapcol = lax.rem(place // 64 + 1, 4) - b
        spot = onehot(
            (tapcol >= 0)
            & (tapcol <= 2)
            & (iota((192, 256), 0) == tapcol * 64 + lax.rem(place, 64))
        )
        for lift in range(3):
            block = nn(decode_fine[lift], spot).astype(BF16)
            final = nn(w_leave[lift], spot)
            for a in (0, 1):
                first, second = WINDOW[a + lift]
                rows = slice(a * 128 + b * 64, a * 128 + b * 64 + 64)
                w_df[rows, first : first + 128] = block[:, 0:128]
                w_df[rows, second : second + 128] = block[:, 128:256]
                rows = slice(b * 8 + a * 3, b * 8 + a * 3 + 3)
                leavef[rows, first : first + 128] = final[:, 0:128]
                leavef[rows, second : second + 128] = final[:, 128:256]
    w_lv[144:160, :] = leavef[...].astype(BF16)

    total = None
    for k in range(4):
        spot = onehot(iota((64, 256), 1) == iota((64, 256), 0) + 64 * k)
        term = nn(pool_fine[k], spot)
        total = term if total is None else total + term
    w_pf[...] = total.astype(BF16)
    for k in range(4):
        w_pm[:, k * 128 : k * 128 + 128] = pool_mid[k]
    has_before = (p > 0).astype(F32)
    has_after = (p < planes - 1).astype(F32)
    w_ac[:, 0:128] = (w_across[0].astype(F32) * has_before).astype(BF16)
    w_ac[:, 128:256] = w_across[1]
    w_ac[:, 256:384] = (w_across[2].astype(F32) * has_after).astype(BF16)
    w_dm[...] = jnp.zeros_like(w_dm)
    for b in (0, 1):
        for lift in range(3):
            for step in range(3):
                spot = 512 * lift + 128 * ((b + step + 3) % 4)
                w_dm[b * 128 : b * 128 + 128, spot : spot + 128] = decode_mid[
                    lift, :, step * 128 : step * 128 + 128
                ]

    for a in (0, 1):
        for b in (0, 1):
            total = None
            for lift in range(3):
                k = iota((18, 1024), 0)
                tgt = (k // 6 + b) * 256 + (a + lift) * 8 + lax.rem(k, 6)
                term = nn(w_enter[lift], onehot(iota((18, 1024), 1) == tgt))
                total = term if total is None else total + term
            tapf[a * 128 + b * 64 : a * 128 + b * 64 + 64, :] = total

    def band(x, carry):
        for wc in range(4):
            lanes = slice(wc * 256, wc * 256 + 256)
            w_in[x, :, lanes] = pltpu.roll(tapf[0:256, lanes], 16 * x, 1).astype(BF16)
        return carry

    lax.fori_loop(0, 10, band, 0)

    shape = (5, 9, 16, 256)
    block = iota(shape, 2)
    row = (block // 4) * 5 + iota(shape, 0) - 2
    col = lax.rem(block, 4) * 9 + iota(shape, 1) - 2
    low_row, high_row = jnp.where(h == 0, 0, -9), jnp.where(h == heights - 1, 16, 99)
    low_col, high_col = jnp.where(s == 0, 0, -9), jnp.where(s == spans - 1, 32, 99)
    inside = (row >= low_row) & (row < high_row) & (col >= low_col) & (col < high_col)
    mask[...] = jnp.where(inside, 1.0, 0.0)

    for k in range(1, planes):
        copy_p(k).wait()
    planef[...] = jnp.zeros_like(planef)
    total = got_p[0].astype(F32)
    for k in range(1, planes):
        total = total + got_p[k].astype(F32)
    planef[:, 2:34, :] = total
    heightf[...] = jnp.zeros_like(heightf)
    for k in range(heights):
        for c in range(3):
            heightf[k, 12 * c : 12 * c + 12, :] = planef[c, 8 * k : 8 * k + 12, :]
    send_h[...] = heightf[...].astype(BF16)

    def copy_h(k):
        return remote(send_h.at[lax.rem(h + k, heights)], got_h.at[h], sem_h, (k,), (0, 0, k))

    for k in range(1, heights):
        copy_h(k).start()
    got_h[h] = send_h[h]

    for copy in halo:
        copy.wait()
    around[1, :, 16:80, :] = noisy[0]
    row = iota((96, 128), 0)
    rows_in = jnp.where((row >= jnp.where(h == 0, 16, 0)) & (row < jnp.where(h == heights - 1, 80, 96)), 1.0, 0.0)
    right = rows_in * (s < spans - 1).astype(F32)
    left = rows_in * (s > 0).astype(F32)
    near = iota((96, 128), 1) < 64
    entryf[...] = jnp.zeros_like(entryf)
    for c in range(3):
        aroundf[0] = around[1, c].astype(F32) * rows_in
        aroundf[1] = jnp.where(
            near, around[2, c].astype(F32) * right, around[0, c].astype(F32) * left
        )
        for rb in range(4):
            for part in range(2):
                entryf[2 * rb + part, pl.ds(c, 22, stride=8), :] = aroundf[
                    part, 7 + 20 * rb : 29 + 20 * rb, :
                ]
    entry = jnp.concatenate([entryf[k] for k in range(8)], axis=1).astype(BF16)
    line = iota((288, 1), 0)
    block = lax.rem(line, 16)
    cell = 36 * lax.rem(block, 4) + 2 * (line // 16) - 9
    for wc in range(4):
        tgt = (block // 4) * 256 + ((cell + wc) & 255)
        tapf[:, wc * 256 : wc * 256 + 256] = nt(onehot(iota((288, 1024), 1) == tgt), entry)

    for k in range(1, heights):
        copy_h(k).wait()
    total = got_h[0].astype(F32)
    for k in range(1, heights):
        total = total + got_h[k].astype(F32)
    rowsf[...] = total

    def window(k):
        dest = lax.rem(s + k, spans)
        lane = iota((8, 128), 1)
        total = jnp.zeros((8, 128), F32)
        for g in range(5):
            shift = lax.rem(24 * g + 2 - 16 * dest + 512, 256)
            moved = pltpu.roll(rowsf[8 * g : 8 * g + 8, :], shift, 1)[:, 0:128]
            total = jnp.where((lane >= 24 * g) & (lane < 24 * g + 20), moved, total)
        return total.astype(BF16)

    def copy_s(k):
        return remote(send_s.at[k], got_s.at[s], sem_s, (k,), (0, k, 0))

    def push(k, carry):
        send_s[k] = window(k)
        copy_s(k).start()
        return carry

    lax.fori_loop(1, spans, push, 0)
    got_s[s] = window(0)

    def take(k, carry):
        copy_s(k).wait()
        return carry

    lax.fori_loop(1, spans, take, 0)
    total = got_s[0].astype(F32)
    for k in range(1, spans):
        total = total + got_s[k].astype(F32)
    lane = iota((8, 128), 1)
    spot = lane - 24 * (lane // 24)
    outside = ((spot < 2) & (s == 0)) | ((spot >= 18) & (s == spans - 1))
    total = jnp.where(outside, 0.0, total)
    for g in range(5):
        part = total if g == 0 else pltpu.roll(total, 128 - 24 * g, 1)
        part = jnp.where(lane < 20, part, 0.0)
        for rb in range(4):
            condf[rb * 40 + 8 * g : rb * 40 + 8 * g + 8, :] = (
                part if rb == 0 else pltpu.roll(part, 32 * rb, 1)
            )
    line = iota((256, 160), 0)
    channel = lax.rem(line, 8) - 3
    m = iota((256, 160), 1)
    rb = m // 40
    tgt = channel * 12 + (rb * 20 + line // 8 + 7) // 8
    pick = (channel >= 0) & (channel < 3) & (line < 176) & (m - 40 * rb == tgt)
    lifted = nn(onehot(pick), condf[...].astype(BF16)).astype(BF16)
    line = iota((288, 1), 0)
    block = lax.rem(line, 16)
    cell = 36 * lax.rem(block, 4) + 2 * (line // 16) - 9
    for wc in range(4):
        tgt = (block // 4) * 32 + (cell + wc + 16) // 8
        lanes = slice(wc * 256, wc * 256 + 256)
        tap[:, lanes] = (
            tapf[:, lanes] + nt(onehot(iota((288, 128), 1) == tgt), lifted)
        ).astype(BF16)

    def copy_x(i, way):
        side = 0 if way == 1 else 2
        return remote(sq.at[1, i], sq.at[side, i], sem_x, (0 if way == 1 else 1, i), (way, 0, 0))

    def encode(i, carry):
        for a in (0, 1):
            x = 2 * i + a
            v = silu(nt(tap[...], w_in[x]) + bias[0:1, 0:256]).astype(BF16)
            h1[x] = v.reshape(9, 2, 16, 256)
            v = silu(nt(v, w_pf[...]) + bias[0:1, 256:384]).astype(BF16).reshape(9, 2, 16, 128)
            d1[x, :, :, 0:128] = v[:, 0]
            d1[x, :, :, 128:256] = v[:, 1]
        v = jnp.concatenate(
            [d1[2 * i].reshape(144, 256), d1[2 * i + 1].reshape(144, 256)], axis=1
        )
        v = silu(nt(v, w_pm[...]) + bias[0:1, 384:640]).astype(BF16)
        d2[i] = v.reshape(9, 16, 256)
        sq[1, i] = nt(v, w_squeeze[...]).astype(BF16).reshape(9, 16, 128)
        copy_x(i, 1).start()
        copy_x(i, -1).start()
        return carry

    lax.fori_loop(0, 5, encode, 0)

    def across(i, carry):
        copy_x(i, 1).wait()
        copy_x(i, -1).wait()
        v = jnp.concatenate([sq[t, i].reshape(144, 128) for t in range(3)], axis=1)
        v = nt(v, w_ac[...]).reshape(9, 16, 256) + d2[i].astype(F32)
        mx[i + 1, 1:10] = (v * mask[i]).astype(BF16)
        return carry

    lax.fori_loop(0, 5, across, 0)
    mx[1:6, 0] = roll_rows(mx[1:6, 9], 1)
    mx[1:6, 10] = roll_rows(mx[1:6, 1], 15)
    mx[0] = roll_rows(mx[5], 4)
    mx[6] = roll_rows(mx[1], 12)

    total = None
    for lift in range(3):
        v = jnp.concatenate(
            [mx[lift : lift + 5, step : step + 9].reshape(720, 256) for step in range(3)], axis=1
        )
        term = nt(v, w_middle[lift])
        total = term if total is None else total + term
    c3[...] = silu(total).astype(BF16).reshape(5, 9, 16, 256)

    def lift_mid(i, carry):
        v = nt(c3[i].reshape(144, 256), rise_mid[...].reshape(512, 256))
        for a in (0, 1):
            x = 2 * i + a
            u = v[:, a * 256 : a * 256 + 256].reshape(9, 16, 256) + d1[x].astype(F32)
            v2[x + 1, 1:10] = (u * mask[i]).astype(BF16)
        return carry

    lax.fori_loop(0, 5, lift_mid, 0)
    v2[1:11, 0, :, 128:256] = roll_rows(v2[1:11, 9, :, 128:256], 1)
    v2[1:11, 10, :, 0:128] = roll_rows(v2[1:11, 1, :, 0:128], 15)
    v2[0] = roll_rows(v2[10], 4)
    v2[11] = roll_rows(v2[1], 12)

    def decode_two(i, carry):
        parts = []
        for lift in range(3):
            rows = pl.ds(2 * i + lift, 2)
            parts.append(v2[rows, 1:10].reshape(288, 256))
            parts.append(v2[rows, 2:11, :, 0:128].reshape(288, 128))
            parts.append(v2[rows, 0:9, :, 128:256].reshape(288, 128))
        v = silu(nt(jnp.concatenate(parts, axis=1), w_dm[...])).astype(BF16)
        weight = rise_fine[...].reshape(256, 128)
        for b in (0, 1):
            u = nt(v[:, b * 128 : b * 128 + 128], weight).reshape(2, 9, 16, 256)
            u = u + h1[pl.ds(2 * i, 2), :, b].astype(F32)
            put_phases(f1m, f1s, pl.ds(2 * i + 1, 2), b, (u * mask[i]).astype(BF16))
        return carry

    lax.fori_loop(0, 5, decode_two, 0)
    close_phases(f1m, f1s)

    def decode_one(x, carry):
        v = silu(nt(phase_window(f1m, f1s, x), w_df[...])).reshape(9, 2, 16, 256)
        m = mask[x // 2]
        for b in (0, 1):
            put_phases(f2m, f2s, pl.ds(x + 1, 1), b, (v[:, b] * m).astype(BF16)[None])
        return carry

    lax.fori_loop(0, 10, decode_one, 0)
    close_phases(f2m, f2s)

    acc[...] = jnp.zeros_like(acc)

    def leave(x, carry):
        weight = w_lv[pl.ds(pl.multiple_of(144 - 16 * x, 16), 256), :]
        acc[...] += nt(phase_window(f2m, f2s, x), weight)
        return carry

    lax.fori_loop(0, 10, leave, 0)

    turned[...] = acc[...].T.reshape(16, 2, 8, 288)
    total = None
    for b in (0, 1):
        line = iota((288, 512), 0)
        lane = iota((288, 512), 1)
        block = lax.rem(line, 16)
        tgt = 36 * lax.rem(block, 4) + 2 * (line // 16) + b - 8
        spot = onehot((block // 4 == lane // 128) & (tgt == lax.rem(lane, 128)))
        term = nn(turned[0:10, b].reshape(80, 288).astype(BF16), spot)
        total = term if total is None else total + term
    for rb in range(4):
        outf[rb] = total[:, rb * 128 : rb * 128 + 128]
    for rb in range(4):
        begin, end = max(0, 4 - 10 * rb), min(10, 36 - 10 * rb)
        for a in (0, 1):
            for o in range(3):
                guess[o, pl.ds(20 * rb + 2 * begin + a - 8, end - begin, stride=2), :] = outf[
                    rb, pl.ds(8 * begin + 3 * a + o, end - begin, stride=8), :
                ]
    noise_out[0] = guess[...].astype(BF16)
    now = plan_of(now_step)[0:1, :]
    prior = plan_of(now_step - STRIDE)[0:1, :]
    for c in range(3):
        sample = noisy[0, c].astype(F32)
        clean = (sample - jnp.sqrt(1.0 - now) * guess[c]) / jnp.sqrt(now)
        next_out[0, c] = jnp.sqrt(prior) * clean + jnp.sqrt(1.0 - prior) * guess[c]


def solution(mesh):
    sizes = tuple(mesh.shape[a] for a in ("plane", "span", "height"))
    planes, spans, heights = sizes

    def shards(*args):
        in_vmem = pl.BlockSpec(memory_space=pltpu.VMEM)
        in_smem = pl.BlockSpec(memory_space=pltpu.SMEM)
        vmem = pltpu.VMEM
        scratch = [
            vmem((planes, 3, 32, 256), BF16),
            vmem((planes, 3, 32, 256), BF16),
            vmem((3, 40, 256), F32),
            vmem((heights, 48, 256), F32),
            vmem((heights, 48, 256), BF16),
            vmem((heights, 48, 256), BF16),
            vmem((48, 256), F32),
            vmem((spans, 8, 128), BF16),
            vmem((spans, 8, 128), BF16),
            vmem((3, 3, 96, 128), BF16),
            vmem((2, 96, 128), F32),
            vmem((8, 256, 128), F32),
            vmem((288, 1024), F32),
            vmem((288, 1024), BF16),
            vmem((160, 128), F32),
            vmem((8, 640), F32),
            vmem((10, 256, 1024), BF16),
            vmem((128, 256), BF16),
            vmem((256, 512), BF16),
            vmem((256, 384), BF16),
            vmem((256, 1536), BF16),
            vmem((256, 1024), BF16),
            vmem((16, 1024), F32),
            vmem((400, 1024), BF16),
            vmem((5, 9, 16, 256), F32),
            vmem((10, 9, 2, 16, 256), BF16),
            vmem((10, 9, 16, 256), BF16),
            vmem((5, 9, 16, 256), BF16),
            vmem((3, 5, 9, 16, 128), BF16),
            vmem((7, 11, 16, 256), BF16),
            vmem((5, 9, 16, 256), BF16),
            vmem((12, 11, 16, 256), BF16),
            vmem((12, 9, 2, 16, 256), BF16),
            vmem((12, 11, 2, 16, 256), BF16),
            vmem((12, 9, 2, 16, 256), BF16),
            vmem((12, 11, 2, 16, 256), BF16),
            vmem((288, 256), F32),
            vmem((16, 2, 8, 288), F32),
            vmem((4, 80, 128), F32),
            vmem((3, 64, 128), F32),
            pltpu.SemaphoreType.DMA((2, planes)),
            pltpu.SemaphoreType.DMA((2, heights)),
            pltpu.SemaphoreType.DMA((2, spans)),
            pltpu.SemaphoreType.DMA((2, 8)),
            pltpu.SemaphoreType.DMA((2, 2, 5)),
        ]
        return pl.pallas_call(
            lambda *refs: body(sizes, *refs),
            out_shape=(
                jax.ShapeDtypeStruct((1, 3, 64, 128), BF16),
                jax.ShapeDtypeStruct((1, 3, 64, 128), F32),
            ),
            in_specs=[in_vmem, in_vmem, in_smem, in_smem] + [in_vmem] * 13,
            out_specs=(in_vmem, in_vmem),
            scratch_shapes=scratch,
            compiler_params=pltpu.CompilerParams(
                collective_id=0, has_side_effects=True, vmem_limit_bytes=56 * 1024 * 1024
            ),
            name="denoise",
        )(*args)

    in_specs = (
        P("plane", None, "height", "span"),
        P(("plane", "span", "height"), None, None, None, None),
    ) + (P(),) * 15
    out_specs = (P("plane", None, "height", "span"), P("plane", None, "height", "span"))
    return jax.shard_map(shards, mesh=mesh, in_specs=in_specs, out_specs=out_specs, check_vma=False)
```

```python
import math

import jax
import jax.numpy as jnp
from jax import lax
from jax.experimental import pallas as pl
from jax.experimental.pallas import tpu as pltpu
from jax.sharding import PartitionSpec as P

TSTEPS = 1000
STRIDE = 20
F32 = jnp.float32
BF16 = jnp.bfloat16
MESH = pl.DeviceIdType.MESH
HIGHEST = lax.Precision.HIGHEST


def nt(a, b):
    return lax.dot_general(a, b, (((1,), (1,)), ((), ())), preferred_element_type=F32)


def nn(a, b):
    return lax.dot_general(a, b, (((1,), (0,)), ((), ())), preferred_element_type=F32)


def tn(a, b):
    return lax.dot_general(a, b, (((0,), (0,)), ((), ())), preferred_element_type=F32)


def silu(v):
    return v * (0.5 * jnp.tanh(0.5 * v) + 0.5)


def iota(shape, dim):
    return lax.broadcasted_iota(jnp.int32, shape, dim)


def onehot(cond):
    return jnp.where(cond, 1.0, 0.0).astype(BF16)


def roll_rows(v, shift):
    return pltpu.roll(v.astype(F32), shift, v.ndim - 2).astype(BF16)


def plan_of(step):
    phase = (step / TSTEPS + 0.008) / 1.008 * (math.pi / 2.0)
    return jnp.cos(phase) ** 2


WINDOW = ((0, 128), (256, 512), (384, 640), (768, 896))


def phase_window(main, side, x, n):
    def flat(v):
        return v.reshape(n * 288, v.shape[-1])

    above, here, below = slice(x, x + n), slice(x + 1, x + 1 + n), slice(x + 2, x + 2 + n)
    return jnp.concatenate(
        [
            flat(main[above, :, :, :, 128:256]),
            flat(side[above, 1:10, :, :, 128:256]),
            flat(main[here]),
            flat(side[here, 1:10]),
            flat(main[below, :, :, :, 0:128]),
            flat(side[below, 1:10, :, :, 0:128]),
        ],
        axis=1,
    )


def put_phases(main, side, rows, b, v):
    main[rows, :, b] = v
    below, above = (slice(1, 10), slice(2, 11)) if b else (slice(0, 9), slice(1, 10))
    for low in (0, 128):
        side[rows, below, 1 - b, :, low : low + 64] = v[..., low : low + 64]
        side[rows, above, 1 - b, :, low + 64 : low + 128] = v[..., low + 64 : low + 128]


def close_phases(main, side):
    right = roll_rows(main[1:11, 8, 1], 1)
    left = roll_rows(main[1:11, 0, 0], 15)
    for low in (0, 128):
        side[1:11, 1, 0, :, low + 64 : low + 128] = right[..., low + 64 : low + 128]
        side[1:11, 9, 1, :, low : low + 64] = left[..., low : low + 64]
    main[0, :, :, :, 128:256] = roll_rows(main[10, :, :, :, 128:256], 4)
    side[0, 1:10, :, :, 128:256] = roll_rows(side[10, 1:10, :, :, 128:256], 4)
    main[11, :, :, :, 0:128] = roll_rows(main[1, :, :, :, 0:128], 12)
    side[11, 1:10, :, :, 0:128] = roll_rows(side[1, 1:10, :, :, 0:128], 12)


def body(sizes, noisy_hbm, slot_hbm, timestep, owner, *refs):
    weights_hbm, outputs, local, refs = refs[:13], refs[13:16], refs[16:31], refs[31:]
    guess, kept, again = outputs
    slot, noisy, *weights = local
    (w_embed, w_biases, w_enter, pool_fine, pool_mid, w_squeeze, w_across) = weights[:7]
    (w_middle, rise_mid, decode_mid, rise_fine, decode_fine, w_leave) = weights[7:]
    (send_p, got_c, hold, got_p, planef, heightf, send_h, got_h, rowsf, send_s, got_s) = refs[:11]
    (around, aroundf, entryf, tapf, tap, condf, bias, coef, bandf, w_in, w_pf, w_pm) = refs[11:23]
    (w_ac, w_dm, w_df, leavef, w_lv, mask, mask2, h1, d1, d2, sq, mx, c3, v2) = refs[23:37]
    (f1m, f1s, f2m, f2s, turned, outf) = refs[37:43]
    (sem_w, sem_c, sem_p, sem_h, sem_s, sem_n, sem_x) = refs[43:]
    planes, spans, heights = sizes
    p, s, h = (lax.axis_index(a) for a in ("plane", "span", "height"))

    def at(dp, ds, dh):
        return (
            lax.rem(p + (dp + planes), planes),
            lax.rem(s + (ds + spans), spans),
            lax.rem(h + (dh + heights), heights),
        )

    core = lax.rem(p, 2)
    mate = 1 - 2 * core
    chip = p // 2
    chips = planes // 2

    loads = [
        pltpu.make_async_copy(src, dst, sem_w.at[k])
        for k, (src, dst) in enumerate(zip((slot_hbm, noisy_hbm) + weights_hbm, local))
    ]
    for load in loads:
        load.start()

    barrier = pltpu.get_barrier_semaphore()
    partners = [(mate, 0, 0), (-mate, 0, 0)]
    partners += [(2 * k, 0, 0) for k in range(1, chips)]
    partners += [(0, k, 0) for k in range(1, spans)]
    partners += [(0, 0, k) for k in range(1, heights)]
    partners += [(0, ds, dh) for ds in (-1, 1) for dh in (-1, 1)]
    for offset in partners:
        pl.semaphore_signal(barrier, inc=1, device_id=at(*offset), device_id_type=MESH)
    def remote(src, dst, sems, index, offset):
        return pltpu.make_async_remote_copy(
            src_ref=src,
            dst_ref=dst,
            send_sem=sems.at[(0,) + index],
            recv_sem=sems.at[(1,) + index],
            device_id=at(*offset),
            device_id_type=MESH,
        )

    loads[0].wait()
    loads[1].wait()
    mine = (owner[0] == (p * spans + s) * heights + h).astype(F32)
    for k in range(planes):
        send_p[k % 2, k // 2] = (slot[0, k].astype(F32) * mine).astype(BF16)
    pl.semaphore_wait(barrier, len(partners))
    to_mate = remote(send_p.at[1 - core], got_c, sem_c, (0,), (mate, 0, 0))
    to_mate.start()

    halo = []
    for ds in (-1, 0, 1):
        for dh in (-1, 0, 1):
            if ds == 0 and dh == 0:
                continue
            src = {-1: slice(0, 16), 0: slice(0, 64), 1: slice(48, 64)}[dh]
            dst = {-1: slice(80, 96), 0: slice(16, 80), 1: slice(0, 16)}[dh]
            halo.append(
                remote(
                    noisy.at[0, :, src], around.at[1 - ds, :, dst], sem_n, (len(halo),), (0, ds, dh)
                )
            )
    for copy in halo:
        copy.start()

    to_mate.wait()
    for k in range(chips):
        hold[k] = (send_p[core, k].astype(F32) + got_c[k].astype(F32)).astype(BF16)

    def copy_p(k):
        dest = lax.rem(chip + k, chips)
        return remote(hold.at[dest], got_p.at[chip], sem_p, (k,), (2 * k, 0, 0))

    for k in range(1, chips):
        copy_p(k).start()
    got_p[chip] = hold[chip]
    for load in loads[2:]:
        load.wait()

    now_step = jnp.full((8, 128), timestep[0].astype(F32), F32)
    now = plan_of(now_step)
    prior = plan_of(now_step - STRIDE)
    coef[0] = jnp.sqrt(1.0 - now)
    coef[1] = jnp.sqrt(now)
    coef[2] = jnp.sqrt(prior)
    again[...] = jnp.broadcast_to(jnp.sqrt(1.0 - prior)[0:1], (64, 128))
    lane = iota((8, 64), 1)
    order = jnp.where(lane < 32, lane, lane - 32).astype(F32)
    angle = timestep[0].astype(F32) * jnp.exp(order * (-math.log(10000.0) / 32))
    waves = jnp.where(lane < 32, jnp.sin(angle), jnp.cos(angle))
    hidden = jnp.dot(waves, w_embed[...], precision=HIGHEST, preferred_element_type=F32)
    hidden = hidden / (1.0 + jnp.exp(-hidden))
    flat = lax.dot_general(
        hidden, w_biases[...], (((1,), (1,)), ((), ())), HIGHEST, preferred_element_type=F32
    )
    col = iota((448, 640), 1)
    pick = jnp.where(col < 256, lax.rem(col, 64), col - 192)
    pick = jnp.where(iota((448, 640), 0) == pick, 1.0, 0.0)
    bias[...] = jnp.dot(flat, pick, precision=HIGHEST, preferred_element_type=F32)

    w_df[...] = jnp.zeros_like(w_df)
    w_lv[...] = jnp.zeros_like(w_lv)
    leavef[...] = jnp.zeros_like(leavef)
    for b in (0, 1):
        place = iota((192, 256), 1)
        tapcol = lax.rem(place // 64 + 1, 4) - b
        spot = onehot(
            (tapcol >= 0)
            & (tapcol <= 2)
            & (iota((192, 256), 0) == tapcol * 64 + lax.rem(place, 64))
        )
        for lift in range(3):
            block = nn(decode_fine[lift], spot).astype(BF16)
            final = nn(w_leave[lift], spot)
            for a in (0, 1):
                first, second = WINDOW[a + lift]
                rows = slice(a * 128 + b * 64, a * 128 + b * 64 + 64)
                w_df[rows, first : first + 128] = block[:, 0:128]
                w_df[rows, second : second + 128] = block[:, 128:256]
                rows = slice(b * 8 + a * 3, b * 8 + a * 3 + 3)
                leavef[rows, first : first + 128] = final[:, 0:128]
                leavef[rows, second : second + 128] = final[:, 128:256]
    final = leavef[...].astype(BF16)
    for x in range(10):
        for k, begin in enumerate((0, 128, 256, 512, 384, 640, 768, 896)):
            spot = 512 * x + 128 * k
            w_lv[16 * x : 16 * x + 16, spot : spot + 128] = final[:, begin : begin + 128]

    for k in range(4):
        w_pf[k * 64 : k * 64 + 64, :] = pool_fine[k]
        w_pm[:, k * 128 : k * 128 + 128] = pool_mid[k]
    has_before = (p > 0).astype(F32)
    has_after = (p < planes - 1).astype(F32)
    w_ac[:, 0:128] = (w_across[0].astype(F32) * has_before).astype(BF16)
    w_ac[:, 128:256] = w_across[1]
    w_ac[:, 256:384] = (w_across[2].astype(F32) * has_after).astype(BF16)
    w_dm[...] = jnp.zeros_like(w_dm)
    for b in (0, 1):
        for lift in range(3):
            for step in range(3):
                spot = 512 * lift + 128 * ((b + step + 3) % 4)
                w_dm[b * 128 : b * 128 + 128, spot : spot + 128] = decode_mid[
                    lift, :, step * 128 : step * 128 + 128
                ]

    for a in (0, 1):
        for b in (0, 1):
            total = None
            for lift in range(3):
                k = iota((18, 512), 0)
                tgt = (k // 6 + b) * 128 + (a + lift) * 8 + lax.rem(k, 6)
                term = tn(w_enter[lift], onehot(iota((18, 512), 1) == tgt))
                total = term if total is None else total + term
            bandf[a * 128 + b * 64 : a * 128 + b * 64 + 64, :] = total
    for x in range(7):
        for wc in range(4):
            lanes = slice(wc * 128, wc * 128 + 128)
            v = bandf[:, lanes]
            w_in[x, :, lanes] = (v if x == 0 else pltpu.roll(v, 16 * x, 1)).astype(BF16)

    shape = (5, 9, 16, 256)
    block = iota(shape, 2)
    row = (block // 4) * 5 + iota(shape, 0) - 2
    col = lax.rem(block, 4) * 9 + iota(shape, 1) - 2
    low_row, high_row = jnp.where(h == 0, 0, -9), jnp.where(h == heights - 1, 16, 99)
    low_col, high_col = jnp.where(s == 0, 0, -9), jnp.where(s == spans - 1, 32, 99)
    inside = (row >= low_row) & (row < high_row) & (col >= low_col) & (col < high_col)
    mask[...] = jnp.where(inside, 1.0, 0.0)
    for x in range(10):
        mask2[x] = mask[x // 2]

    for k in range(1, chips):
        copy_p(k).wait()
    planef[...] = jnp.zeros_like(planef)
    total = got_p[0].astype(F32)
    for k in range(1, chips):
        total = total + got_p[k].astype(F32)
    planef[:, 2:34, :] = total
    heightf[...] = jnp.zeros_like(heightf)
    for k in range(heights):
        for c in range(3):
            heightf[k, 12 * c : 12 * c + 12, :] = planef[c, 8 * k : 8 * k + 12, :]
    send_h[...] = heightf[...].astype(BF16)

    def copy_h(k):
        return remote(send_h.at[lax.rem(h + k, heights)], got_h.at[h], sem_h, (k,), (0, 0, k))

    for k in range(1, heights):
        copy_h(k).start()
    got_h[h] = send_h[h]

    for copy in halo:
        copy.wait()
    around[1, :, 16:80, :] = noisy[0]
    row = iota((96, 128), 0)
    rows_in = jnp.where((row >= jnp.where(h == 0, 16, 0)) & (row < jnp.where(h == heights - 1, 80, 96)), 1.0, 0.0)
    right = rows_in * (s < spans - 1).astype(F32)
    left = rows_in * (s > 0).astype(F32)
    near = iota((96, 128), 1) < 64
    entryf[...] = jnp.zeros_like(entryf)
    for c in range(3):
        aroundf[0] = around[1, c].astype(F32) * rows_in
        aroundf[1] = jnp.where(
            near, around[2, c].astype(F32) * right, around[0, c].astype(F32) * left
        )
        for rb in range(4):
            for part in range(2):
                entryf[2 * rb + part, pl.ds(c, 22, stride=8), :] = aroundf[
                    part, 7 + 20 * rb : 29 + 20 * rb, :
                ]
    entry = jnp.concatenate([entryf[k] for k in range(8)], axis=1).astype(BF16)
    line = iota((288, 1), 0)
    block = lax.rem(line, 16)
    cell = 36 * lax.rem(block, 4) + 2 * (line // 16) - 9
    for wc in range(4):
        tgt = (block // 4) * 256 + ((cell + wc) & 255)
        spot = onehot(iota((288, 1024), 1) == tgt)
        for g in range(2):
            tapf[g, :, wc * 128 : wc * 128 + 128] = nt(spot, entry[48 * g : 48 * g + 128])

    for k in range(1, heights):
        copy_h(k).wait()
    total = got_h[0].astype(F32)
    for k in range(1, heights):
        total = total + got_h[k].astype(F32)
    rowsf[...] = total

    lane = iota((8, 128), 1)
    for dest in range(spans):
        total = jnp.zeros((8, 128), F32)
        for g in range(5):
            shift = (24 * g + 2 - 16 * dest) % 256
            v = rowsf[8 * g : 8 * g + 8, :]
            moved = (pltpu.roll(v, shift, 1) if shift else v)[:, 0:128]
            total = jnp.where((lane >= 24 * g) & (lane < 24 * g + 20), moved, total)
        send_s[dest] = total.astype(BF16)

    def copy_s(k):
        return remote(send_s.at[lax.rem(s + k, spans)], got_s.at[s], sem_s, (k,), (0, k, 0))

    for k in range(1, spans):
        copy_s(k).start()
    got_s[s] = send_s[s]

    for k in range(1, spans):
        copy_s(k).wait()
    total = got_s[0].astype(F32)
    for k in range(1, spans):
        total = total + got_s[k].astype(F32)
    lane = iota((8, 128), 1)
    spot = lane - 24 * (lane // 24)
    outside = ((spot < 2) & (s == 0)) | ((spot >= 18) & (s == spans - 1))
    total = jnp.where(outside, 0.0, total)
    for g in range(5):
        part = total if g == 0 else pltpu.roll(total, 128 - 24 * g, 1)
        part = jnp.where(lane < 20, part, 0.0)
        for rb in range(4):
            condf[rb * 40 + 8 * g : rb * 40 + 8 * g + 8, :] = (
                part if rb == 0 else pltpu.roll(part, 32 * rb, 1)
            )
    line = iota((256, 160), 0)
    channel = lax.rem(line, 8) - 3
    m = iota((256, 160), 1)
    rb = m // 40
    tgt = channel * 12 + (rb * 20 + line // 8 + 7) // 8
    pick = (channel >= 0) & (channel < 3) & (line < 176) & (m - 40 * rb == tgt)
    lifted = nn(onehot(pick), condf[...].astype(BF16)).astype(BF16)
    line = iota((288, 1), 0)
    block = lax.rem(line, 16)
    cell = 36 * lax.rem(block, 4) + 2 * (line // 16) - 9
    for wc in range(4):
        tgt = (block // 4) * 32 + (cell + wc + 16) // 8
        spot = onehot(iota((288, 128), 1) == tgt)
        lanes = slice(wc * 128, wc * 128 + 128)
        for g in range(2):
            v = tapf[g, :, lanes] + nt(spot, lifted[48 * g : 48 * g + 128])
            tap[g, :, lanes] = v.astype(BF16)

    def copy_x(i, way):
        side = 0 if way == 1 else 2
        return remote(sq.at[1, i], sq.at[side, i], sem_x, (0 if way == 1 else 1, i), (way, 0, 0))

    for i in range(5):
        for a in (0, 1):
            x = 2 * i + a
            v = nt(tap[x // 5], w_in[x - 3 * (x // 5)])
            v = silu(v + bias[0:1, 0:256]).astype(BF16)
            h1[x] = v.reshape(9, 2, 16, 256)
            v = silu(nn(v, w_pf[...]) + bias[0:1, 256:384]).astype(BF16).reshape(9, 2, 16, 128)
            d1[x, :, :, 0:128] = v[:, 0]
            d1[x, :, :, 128:256] = v[:, 1]
        v = jnp.concatenate(
            [d1[2 * i].reshape(144, 256), d1[2 * i + 1].reshape(144, 256)], axis=1
        )
        v = silu(nt(v, w_pm[...]) + bias[0:1, 384:640]).astype(BF16)
        d2[i] = v.reshape(9, 16, 256)
        sq[1, i] = nt(v, w_squeeze[...]).astype(BF16).reshape(9, 16, 128)
        copy_x(i, 1).start()
        copy_x(i, -1).start()

    for i in range(5):
        copy_x(i, 1).wait()
        copy_x(i, -1).wait()
        v = jnp.concatenate([sq[t, i].reshape(144, 128) for t in range(3)], axis=1)
        v = nt(v, w_ac[...]).reshape(9, 16, 256) + d2[i].astype(F32)
        mx[i + 1, 1:10] = (v * mask[i]).astype(BF16)
    mx[1:6, 0] = roll_rows(mx[1:6, 9], 1)
    mx[1:6, 10] = roll_rows(mx[1:6, 1], 15)
    mx[0] = roll_rows(mx[5], 4)
    mx[6] = roll_rows(mx[1], 12)

    total = None
    for lift in range(3):
        v = jnp.concatenate(
            [mx[lift : lift + 5, step : step + 9].reshape(720, 256) for step in range(3)], axis=1
        )
        term = nt(v, w_middle[lift])
        total = term if total is None else total + term
    c3[...] = silu(total).astype(BF16).reshape(5, 9, 16, 256)

    v = nt(c3[...].reshape(720, 256), rise_mid[...].reshape(512, 256)).reshape(5, 9, 16, 512)
    for x in range(10):
        u = v[x // 2, :, :, x % 2 * 256 : x % 2 * 256 + 256] + d1[x].astype(F32)
        v2[x + 1, 1:10] = (u * mask2[x]).astype(BF16)
    v2[1:11, 0, :, 128:256] = roll_rows(v2[1:11, 9, :, 128:256], 1)
    v2[1:11, 10, :, 0:128] = roll_rows(v2[1:11, 1, :, 0:128], 15)
    v2[0] = roll_rows(v2[10], 4)
    v2[11] = roll_rows(v2[1], 12)

    parts = []
    for lift in range(3):
        rows = slice(lift, lift + 10)
        parts.append(v2[rows, 1:10].reshape(1440, 256))
        parts.append(v2[rows, 2:11, :, 0:128].reshape(1440, 128))
        parts.append(v2[rows, 0:9, :, 128:256].reshape(1440, 128))
    v = silu(nt(jnp.concatenate(parts, axis=1), w_dm[...])).astype(BF16)
    weight = rise_fine[...].reshape(256, 128)
    for b in (0, 1):
        u = nt(v[:, b * 128 : b * 128 + 128], weight).reshape(10, 9, 16, 256)
        u = u + h1[:, :, b].astype(F32)
        put_phases(f1m, f1s, slice(1, 11), b, (u * mask2[...]).astype(BF16))
    close_phases(f1m, f1s)

    for x in range(0, 10, 5):
        v = silu(nt(phase_window(f1m, f1s, x, 5), w_df[...])).reshape(5, 9, 2, 16, 256)
        for b in (0, 1):
            u = (v[:, :, b] * mask2[x : x + 5]).astype(BF16)
            put_phases(f2m, f2s, slice(x + 1, x + 6), b, u)
    close_phases(f2m, f2s)

    parts = []
    for x in range(12):
        for low in (0, 128):
            if (x, low) not in ((0, 0), (11, 128)):
                parts.append(f2m[x, :, :, :, low : low + 128].reshape(288, 128))
                parts.append(f2s[x, 1:10, :, :, low : low + 128].reshape(288, 128))
    out = nt(jnp.concatenate(parts, axis=1), w_lv[...])

    turned[...] = out.T.reshape(16, 2, 8, 288)
    total = None
    for b in (0, 1):
        line = iota((288, 512), 0)
        lane = iota((288, 512), 1)
        block = lax.rem(line, 16)
        tgt = 36 * lax.rem(block, 4) + 2 * (line // 16) + b - 8
        spot = onehot((block // 4 == lane // 128) & (tgt == lax.rem(lane, 128)))
        term = nn(turned[0:10, b].reshape(80, 288).astype(BF16), spot)
        total = term if total is None else total + term
    for rb in range(4):
        outf[rb] = total[:, rb * 128 : rb * 128 + 128]
    for rb in range(4):
        begin, end = max(0, 4 - 10 * rb), min(10, 36 - 10 * rb)
        for a in (0, 1):
            for o in range(3):
                guess[o, pl.ds(20 * rb + 2 * begin + a - 8, end - begin, stride=2), :] = outf[
                    rb, pl.ds(8 * begin + 3 * a + o, end - begin, stride=8), :
                ]
    for c in range(3):
        clean = (noisy[0, c].astype(F32) - coef[0, 0:1] * guess[c]) / coef[1, 0:1]
        kept[c] = coef[2, 0:1] * clean


def solution(mesh):
    sizes = tuple(mesh.shape[a] for a in ("plane", "span", "height"))
    planes, spans, heights = sizes

    def shards(*args):
        args = list(args)
        args[5] = args[5].T
        args[6] = args[6].transpose(0, 2, 1)
        args[7] = args[7].transpose(0, 2, 1)
        in_vmem = pl.BlockSpec(memory_space=pltpu.VMEM)
        in_smem = pl.BlockSpec(memory_space=pltpu.SMEM)
        in_any = pl.BlockSpec(memory_space=pl.ANY)
        vmem = pltpu.VMEM
        order = [1, 0] + list(range(4, 17))
        scratch = [vmem(args[k].shape, args[k].dtype) for k in order] + [
            vmem((2, planes // 2, 3, 32, 256), BF16),
            vmem((planes // 2, 3, 32, 256), BF16),
            vmem((planes // 2, 3, 32, 256), BF16),
            vmem((planes // 2, 3, 32, 256), BF16),
            vmem((3, 40, 256), F32),
            vmem((heights, 48, 256), F32),
            vmem((heights, 48, 256), BF16),
            vmem((heights, 48, 256), BF16),
            vmem((48, 256), F32),
            vmem((spans, 8, 128), BF16),
            vmem((spans, 8, 128), BF16),
            vmem((3, 3, 96, 128), BF16),
            vmem((2, 96, 128), F32),
            vmem((8, 256, 128), F32),
            vmem((2, 288, 512), F32),
            vmem((2, 288, 512), BF16),
            vmem((160, 128), F32),
            vmem((8, 640), F32),
            vmem((3, 8, 128), F32),
            vmem((256, 512), F32),
            vmem((7, 256, 512), BF16),
            vmem((256, 128), BF16),
            vmem((256, 512), BF16),
            vmem((256, 384), BF16),
            vmem((256, 1536), BF16),
            vmem((256, 1024), BF16),
            vmem((16, 1024), F32),
            vmem((256, 5632), BF16),
            vmem((5, 9, 16, 256), F32),
            vmem((10, 9, 16, 256), F32),
            vmem((10, 9, 2, 16, 256), BF16),
            vmem((10, 9, 16, 256), BF16),
            vmem((5, 9, 16, 256), BF16),
            vmem((3, 5, 9, 16, 128), BF16),
            vmem((7, 11, 16, 256), BF16),
            vmem((5, 9, 16, 256), BF16),
            vmem((12, 11, 16, 256), BF16),
            vmem((12, 9, 2, 16, 256), BF16),
            vmem((12, 11, 2, 16, 256), BF16),
            vmem((12, 9, 2, 16, 256), BF16),
            vmem((12, 11, 2, 16, 256), BF16),
            vmem((16, 2, 8, 288), F32),
            vmem((4, 80, 128), F32),
            pltpu.SemaphoreType.DMA((15,)),
            pltpu.SemaphoreType.DMA((2, 1)),
            pltpu.SemaphoreType.DMA((2, planes // 2)),
            pltpu.SemaphoreType.DMA((2, heights)),
            pltpu.SemaphoreType.DMA((2, spans)),
            pltpu.SemaphoreType.DMA((2, 8)),
            pltpu.SemaphoreType.DMA((2, 2, 5)),
        ]
        guess, kept, again = pl.pallas_call(
            lambda *refs: body(sizes, *refs),
            out_shape=(
                jax.ShapeDtypeStruct((3, 64, 128), F32),
                jax.ShapeDtypeStruct((3, 64, 128), F32),
                jax.ShapeDtypeStruct((64, 128), F32),
            ),
            in_specs=[in_any, in_any, in_smem, in_smem] + [in_any] * 13,
            out_specs=(in_vmem, in_vmem, in_vmem),
            scratch_shapes=scratch,
            compiler_params=pltpu.CompilerParams(
                collective_id=0, has_side_effects=True, vmem_limit_bytes=56 * 1024 * 1024
            ),
            name="denoise",
        )(*args)
        return guess[None].astype(BF16), (kept + again * guess)[None]

    in_specs = (
        P("plane", None, "height", "span"),
        P(("plane", "span", "height"), None, None, None, None),
    ) + (P(),) * 15
    out_specs = (P("plane", None, "height", "span"), P("plane", None, "height", "span"))
    return jax.shard_map(shards, mesh=mesh, in_specs=in_specs, out_specs=out_specs, check_vma=False)
```

```python
import math

import jax
import jax.numpy as jnp
from jax import lax
from jax.experimental import pallas as pl
from jax.experimental.pallas import tpu as pltpu
from jax.sharding import PartitionSpec as P

TSTEPS = 1000
STRIDE = 20
F32 = jnp.float32
BF16 = jnp.bfloat16
MESH = pl.DeviceIdType.MESH
HIGHEST = lax.Precision.HIGHEST


def nt(a, b):
    return lax.dot_general(a, b, (((1,), (1,)), ((), ())), preferred_element_type=F32)


def nn(a, b):
    return lax.dot_general(a, b, (((1,), (0,)), ((), ())), preferred_element_type=F32)


def tn(a, b):
    return lax.dot_general(a, b, (((0,), (0,)), ((), ())), preferred_element_type=F32)


def silu(v):
    return v * (0.5 * jnp.tanh(0.5 * v) + 0.5)


def iota(shape, dim):
    return lax.broadcasted_iota(jnp.int32, shape, dim)


def onehot(cond):
    return jnp.where(cond, 1.0, 0.0).astype(BF16)


def roll_rows(v, shift):
    return pltpu.roll(v.astype(F32), shift, v.ndim - 2).astype(BF16)


def plan_of(step):
    phase = (step / TSTEPS + 0.008) / 1.008 * (math.pi / 2.0)
    return jnp.cos(phase) ** 2


WINDOW = ((0, 128), (256, 512), (384, 640), (768, 896))


def phase_window(main, side, x, n):
    def flat(v):
        return v.reshape(n * 288, v.shape[-1])

    above, here, below = slice(x, x + n), slice(x + 1, x + 1 + n), slice(x + 2, x + 2 + n)
    return jnp.concatenate(
        [
            flat(main[above, :, :, :, 128:256]),
            flat(side[above, 1:10, :, :, 128:256]),
            flat(main[here]),
            flat(side[here, 1:10]),
            flat(main[below, :, :, :, 0:128]),
            flat(side[below, 1:10, :, :, 0:128]),
        ],
        axis=1,
    )


def put_phases(main, side, x, b, v):
    rows = slice(x + 1, x + 1 + v.shape[0])
    below, above = (slice(1, 10), slice(2, 11)) if b else (slice(0, 9), slice(1, 10))
    edge = pltpu.roll(v[:, 8], 1, 1) if b else pltpu.roll(v[:, 0], 15, 1)
    v, edge = v.astype(BF16), edge.astype(BF16)
    main[rows, :, b] = v
    for low in (0, 128):
        side[rows, below, 1 - b, :, low : low + 64] = v[..., low : low + 64]
        side[rows, above, 1 - b, :, low + 64 : low + 128] = v[..., low + 64 : low + 128]
    for low in (0, 128):
        if b:
            side[rows, 1, 0, :, low + 64 : low + 128] = edge[..., low + 64 : low + 128]
        else:
            side[rows, 9, 1, :, low : low + 64] = edge[..., low : low + 64]


def close_below(main, side):
    main[11, :, :, :, 0:128] = roll_rows(main[1, :, :, :, 0:128], 12)
    side[11, 1:10, :, :, 0:128] = roll_rows(side[1, 1:10, :, :, 0:128], 12)


def close_above(main, side):
    main[0, :, :, :, 128:256] = roll_rows(main[10, :, :, :, 128:256], 4)
    side[0, 1:10, :, :, 128:256] = roll_rows(side[10, 1:10, :, :, 128:256], 4)


def body(sizes, noisy_hbm, slot_hbm, timestep, owner, *refs):
    weights_hbm, outputs, local, refs = refs[:13], refs[13:16], refs[16:31], refs[31:]
    guess, kept, again = outputs
    slot, noisy, *weights = local
    (w_embed, w_biases, w_enter, pool_fine, pool_mid, w_squeeze, w_across) = weights[:7]
    (w_middle, rise_mid, decode_mid, rise_fine, decode_fine, w_leave) = weights[7:]
    (send_p, got_c, planef, heightf, send_h, got_h, rowsf, send_s, got_s) = refs[:9]
    refs = refs[9:]
    (around, aroundf, entryf, tapf, tap, condf, bias, coef, bandf, w_in, w_pf, w_pm) = refs[:12]
    (w_ac, w_dm, w_df, leavef, w_lv, mask, mask2, h1, d1, d2, sq, mx, c3, v2) = refs[12:26]
    (f1m, f1s, f2m, f2s, turned, outf) = refs[26:32]
    (sem_w, sem_c, sem_h, sem_s, sem_n, sem_x) = refs[32:]
    planes, spans, heights = sizes
    p, s, h = (lax.axis_index(a) for a in ("plane", "span", "height"))

    def at(dp, ds, dh):
        return (
            lax.rem(p + (dp + planes), planes),
            lax.rem(s + (ds + spans), spans),
            lax.rem(h + (dh + heights), heights),
        )

    core = lax.rem(p, 2)
    mate = 1 - 2 * core
    chip = p // 2
    chips = planes // 2

    loads = [
        pltpu.make_async_copy(src, dst, sem_w.at[k])
        for k, (src, dst) in enumerate(zip((slot_hbm, noisy_hbm) + weights_hbm, local))
    ]
    for load in loads:
        load.start()

    barrier = pltpu.get_barrier_semaphore()
    partners = [(mate, 0, 0), (-mate, 0, 0)]
    partners += [(2 * j, 0, k) for j in range(chips) for k in range(heights) if j or k]
    partners += [(0, k, 0) for k in range(1, spans)]
    partners += [(0, ds, dh) for ds in (-1, 1) for dh in (-1, 1)]
    for offset in partners:
        pl.semaphore_signal(barrier, inc=1, device_id=at(*offset), device_id_type=MESH)
    def remote(src, dst, sems, index, offset):
        return pltpu.make_async_remote_copy(
            src_ref=src,
            dst_ref=dst,
            send_sem=sems.at[(0,) + index],
            recv_sem=sems.at[(1,) + index],
            device_id=at(*offset),
            device_id_type=MESH,
        )

    loads[0].wait()
    loads[1].wait()
    mine = (owner[0] == (p * spans + s) * heights + h).astype(F32)
    for k in range(planes):
        send_p[k % 2, k // 2] = (slot[0, k].astype(F32) * mine).astype(BF16)
    pl.semaphore_wait(barrier, len(partners))
    to_mate = remote(send_p.at[1 - core], got_c, sem_c, (0,), (mate, 0, 0))
    to_mate.start()

    halo = []
    for ds in (-1, 0, 1):
        for dh in (-1, 0, 1):
            if ds == 0 and dh == 0:
                continue
            src = {-1: slice(0, 16), 0: slice(0, 64), 1: slice(48, 64)}[dh]
            dst = {-1: slice(80, 96), 0: slice(16, 80), 1: slice(0, 16)}[dh]
            halo.append(
                remote(
                    noisy.at[0, :, src], around.at[1 - ds, :, dst], sem_n, (len(halo),), (0, ds, dh)
                )
            )
    for copy in halo:
        copy.start()

    heightf[...] = jnp.zeros_like(heightf)
    to_mate.wait_recv()
    planef[...] = jnp.zeros_like(planef)
    for j in range(chips):
        planef[j, :, 2:34, :] = send_p[core, j].astype(F32) + got_c[j].astype(F32)
    for j in range(chips):
        for k in range(heights):
            for c in range(3):
                heightf[12 * c : 12 * c + 12, :] = planef[j, c, 8 * k : 8 * k + 12, :]
            send_h[j, k] = heightf[0:40, :].reshape(5, 8, 256).astype(BF16)

    def copy_h(j, k):
        src = send_h.at[lax.rem(chip + j, chips), lax.rem(h + k, heights)]
        return remote(src, got_h.at[chip, h], sem_h, (j, k), (2 * j, 0, k))

    rest = [(j, k) for j in (2, 1, 3, 0) for k in (2, 1, 3, 0) if (j, k) != (0, 0)]
    rest = [(j, k) for j, k in rest if j < chips and k < heights]
    for j, k in rest:
        copy_h(j, k).start()
    got_h[chip, h] = send_h[chip, h]
    for load in loads[2:]:
        load.wait()

    now_step = jnp.full((8, 128), timestep[0].astype(F32), F32)
    now = plan_of(now_step)
    prior = plan_of(now_step - STRIDE)
    coef[0] = jnp.sqrt(1.0 - now)
    coef[1] = jnp.sqrt(now)
    coef[2] = jnp.sqrt(prior)
    again[...] = jnp.broadcast_to(jnp.sqrt(1.0 - prior)[0:1], (64, 128))
    lane = iota((8, 64), 1)
    order = jnp.where(lane < 32, lane, lane - 32).astype(F32)
    angle = timestep[0].astype(F32) * jnp.exp(order * (-math.log(10000.0) / 32))
    waves = jnp.where(lane < 32, jnp.sin(angle), jnp.cos(angle))
    hidden = jnp.dot(waves, w_embed[...], precision=HIGHEST, preferred_element_type=F32)
    hidden = hidden / (1.0 + jnp.exp(-hidden))
    flat = lax.dot_general(
        hidden, w_biases[...], (((1,), (1,)), ((), ())), HIGHEST, preferred_element_type=F32
    )
    col = iota((448, 640), 1)
    pick = jnp.where(col < 256, lax.rem(col, 64), col - 192)
    pick = jnp.where(iota((448, 640), 0) == pick, 1.0, 0.0)
    bias[...] = jnp.dot(flat, pick, precision=HIGHEST, preferred_element_type=F32)

    w_df[...] = jnp.zeros_like(w_df)
    w_lv[...] = jnp.zeros_like(w_lv)
    leavef[...] = jnp.zeros_like(leavef)
    for b in (0, 1):
        place = iota((192, 256), 1)
        tapcol = lax.rem(place // 64 + 1, 4) - b
        spot = onehot(
            (tapcol >= 0)
            & (tapcol <= 2)
            & (iota((192, 256), 0) == tapcol * 64 + lax.rem(place, 64))
        )
        for lift in range(3):
            block = nn(decode_fine[lift], spot).astype(BF16)
            final = nn(w_leave[lift], spot)
            for a in (0, 1):
                first, second = WINDOW[a + lift]
                rows = slice(a * 128 + b * 64, a * 128 + b * 64 + 64)
                w_df[rows, first : first + 128] = block[:, 0:128]
                w_df[rows, second : second + 128] = block[:, 128:256]
                rows = slice(b * 8 + a * 3, b * 8 + a * 3 + 3)
                leavef[rows, first : first + 128] = final[:, 0:128]
                leavef[rows, second : second + 128] = final[:, 128:256]
    final = leavef[...].astype(BF16)
    for x in range(10):
        for k, begin in enumerate((0, 128, 256, 512, 384, 640, 768, 896)):
            spot = 512 * x + 128 * k
            w_lv[16 * x : 16 * x + 16, spot : spot + 128] = final[:, begin : begin + 128]

    for k in range(4):
        w_pf[k * 64 : k * 64 + 64, :] = pool_fine[k]
        w_pm[:, k * 128 : k * 128 + 128] = pool_mid[k]
    has_before = (p > 0).astype(F32)
    has_after = (p < planes - 1).astype(F32)
    w_ac[:, 0:128] = (w_across[0].astype(F32) * has_before).astype(BF16)
    w_ac[:, 128:256] = w_across[1]
    w_ac[:, 256:384] = (w_across[2].astype(F32) * has_after).astype(BF16)
    w_dm[...] = jnp.zeros_like(w_dm)
    for b in (0, 1):
        for lift in range(3):
            for step in range(3):
                spot = 512 * lift + 128 * ((b + step + 3) % 4)
                w_dm[b * 128 : b * 128 + 128, spot : spot + 128] = decode_mid[
                    lift, :, step * 128 : step * 128 + 128
                ]

    for a in (0, 1):
        for b in (0, 1):
            total = None
            for lift in range(3):
                k = iota((18, 512), 0)
                tgt = (k // 6 + b) * 128 + (a + lift) * 8 + lax.rem(k, 6)
                term = tn(w_enter[lift], onehot(iota((18, 512), 1) == tgt))
                total = term if total is None else total + term
            bandf[a * 128 + b * 64 : a * 128 + b * 64 + 64, :] = total
    for x in range(7):
        for wc in range(4):
            lanes = slice(wc * 128, wc * 128 + 128)
            v = bandf[:, lanes]
            w_in[x, :, lanes] = (v if x == 0 else pltpu.roll(v, 16 * x, 1)).astype(BF16)

    shape = (5, 9, 16, 256)
    block = iota(shape, 2)
    row = (block // 4) * 5 + iota(shape, 0) - 2
    col = lax.rem(block, 4) * 9 + iota(shape, 1) - 2
    low_row, high_row = jnp.where(h == 0, 0, -9), jnp.where(h == heights - 1, 16, 99)
    low_col, high_col = jnp.where(s == 0, 0, -9), jnp.where(s == spans - 1, 32, 99)
    inside = (row >= low_row) & (row < high_row) & (col >= low_col) & (col < high_col)
    mask[...] = jnp.where(inside, 1.0, 0.0)
    for x in range(10):
        mask2[x] = mask[x // 2]

    for copy in halo:
        copy.wait_recv()
    around[1, :, 16:80, :] = noisy[0]
    row = iota((96, 128), 0)
    rows_in = jnp.where((row >= jnp.where(h == 0, 16, 0)) & (row < jnp.where(h == heights - 1, 80, 96)), 1.0, 0.0)
    right = rows_in * (s < spans - 1).astype(F32)
    left = rows_in * (s > 0).astype(F32)
    near = iota((96, 128), 1) < 64
    entryf[...] = jnp.zeros_like(entryf)
    for c in range(3):
        aroundf[0] = around[1, c].astype(F32) * rows_in
        aroundf[1] = jnp.where(
            near, around[2, c].astype(F32) * right, around[0, c].astype(F32) * left
        )
        for rb in range(4):
            for part in range(2):
                entryf[2 * rb + part, pl.ds(c, 22, stride=8), :] = aroundf[
                    part, 7 + 20 * rb : 29 + 20 * rb, :
                ]
    entry = jnp.concatenate([entryf[k] for k in range(8)], axis=1).astype(BF16)
    line = iota((288, 1), 0)
    block = lax.rem(line, 16)
    cell = 36 * lax.rem(block, 4) + 2 * (line // 16) - 9
    for wc in range(4):
        tgt = (block // 4) * 256 + ((cell + wc) & 255)
        spot = onehot(iota((288, 1024), 1) == tgt)
        for g in range(2):
            tapf[g, :, wc * 128 : wc * 128 + 128] = nt(spot, entry[48 * g : 48 * g + 128])

    for j, k in rest:
        copy_h(j, k).wait_recv()
    total = None
    for j in range(chips):
        for k in range(heights):
            term = got_h[j, k].astype(F32)
            total = term if total is None else total + term
    rowsf[...] = total

    lane = iota((8, 128), 1)
    for dest in range(spans):
        total = jnp.zeros((8, 128), F32)
        for g in range(5):
            shift = (24 * g + 2 - 16 * dest) % 256
            v = rowsf[g]
            moved = (pltpu.roll(v, shift, 1) if shift else v)[:, 0:128]
            total = jnp.where((lane >= 24 * g) & (lane < 24 * g + 20), moved, total)
        send_s[dest] = total.astype(BF16)

    def copy_s(k):
        return remote(send_s.at[lax.rem(s + k, spans)], got_s.at[s], sem_s, (k,), (0, k, 0))

    far = sorted(range(1, spans), key=lambda k: -min(k, spans - k))
    for k in far:
        copy_s(k).start()
    got_s[s] = send_s[s]

    for k in reversed(far):
        copy_s(k).wait_recv()
    total = got_s[0].astype(F32)
    for k in range(1, spans):
        total = total + got_s[k].astype(F32)
    lane = iota((8, 128), 1)
    spot = lane - 24 * (lane // 24)
    outside = ((spot < 2) & (s == 0)) | ((spot >= 18) & (s == spans - 1))
    total = jnp.where(outside, 0.0, total)
    for g in range(5):
        part = total if g == 0 else pltpu.roll(total, 128 - 24 * g, 1)
        part = jnp.where(lane < 20, part, 0.0)
        for rb in range(4):
            condf[rb * 40 + 8 * g : rb * 40 + 8 * g + 8, :] = (
                part if rb == 0 else pltpu.roll(part, 32 * rb, 1)
            )
    line = iota((256, 160), 0)
    channel = lax.rem(line, 8) - 3
    m = iota((256, 160), 1)
    rb = m // 40
    tgt = channel * 12 + (rb * 20 + line // 8 + 7) // 8
    pick = (channel >= 0) & (channel < 3) & (line < 176) & (m - 40 * rb == tgt)
    lifted = nn(onehot(pick), condf[...].astype(BF16)).astype(BF16)
    line = iota((288, 1), 0)
    block = lax.rem(line, 16)
    cell = 36 * lax.rem(block, 4) + 2 * (line // 16) - 9
    for wc in range(4):
        tgt = (block // 4) * 32 + (cell + wc + 16) // 8
        spot = onehot(iota((288, 128), 1) == tgt)
        lanes = slice(wc * 128, wc * 128 + 128)
        for g in range(2):
            v = tapf[g, :, lanes] + nt(spot, lifted[48 * g : 48 * g + 128])
            tap[g, :, lanes] = v.astype(BF16)

    def copy_x(i, way):
        side = 0 if way == 1 else 2
        return remote(sq.at[1, i], sq.at[side, i], sem_x, (0 if way == 1 else 1, i), (way, 0, 0))

    for i in (0, 4, 1, 2, 3):
        for a in (0, 1):
            x = 2 * i + a
            v = nt(tap[x // 5], w_in[x - 3 * (x // 5)])
            v = silu(v + bias[0:1, 0:256]).astype(BF16)
            h1[x] = v.reshape(9, 2, 16, 256)
            v = silu(nn(v, w_pf[...]) + bias[0:1, 256:384]).astype(BF16).reshape(9, 2, 16, 128)
            d1[x, :, :, 0:128] = v[:, 0]
            d1[x, :, :, 128:256] = v[:, 1]
        v = jnp.concatenate(
            [d1[2 * i].reshape(144, 256), d1[2 * i + 1].reshape(144, 256)], axis=1
        )
        v = silu(nt(v, w_pm[...]) + bias[0:1, 384:640]).astype(BF16)
        d2[i] = v.reshape(9, 16, 256)
        sq[1, i] = nt(v, w_squeeze[...]).astype(BF16).reshape(9, 16, 128)
        copy_x(i, 1).start()
        copy_x(i, -1).start()

    for i in (0, 4, 1, 2, 3):
        copy_x(i, 1).wait_recv()
        copy_x(i, -1).wait_recv()
        v = jnp.concatenate([sq[t, i].reshape(144, 128) for t in range(3)], axis=1)
        v = nt(v, w_ac[...]).reshape(9, 16, 256) + d2[i].astype(F32)
        v = v * mask[i]
        mx[i + 1, 1:10] = v.astype(BF16)
        mx[i + 1, 0] = pltpu.roll(v[8], 1, 0).astype(BF16)
        mx[i + 1, 10] = pltpu.roll(v[0], 15, 0).astype(BF16)
        if i == 0:
            mx[6] = roll_rows(mx[1], 12)
        if i == 4:
            mx[0] = roll_rows(mx[5], 4)

    total = None
    for lift in range(3):
        v = jnp.concatenate(
            [mx[lift : lift + 5, step : step + 9].reshape(720, 256) for step in range(3)], axis=1
        )
        term = nt(v, w_middle[lift])
        total = term if total is None else total + term
    c3[...] = silu(total).astype(BF16).reshape(5, 9, 16, 256)

    v = nt(c3[...].reshape(720, 256), rise_mid[...].reshape(512, 256)).reshape(5, 9, 16, 512)
    for x in (0, 9, 1, 2, 3, 4, 5, 6, 7, 8):
        u = v[x // 2, :, :, x % 2 * 256 : x % 2 * 256 + 256] + d1[x].astype(F32)
        u = u * mask2[x]
        v2[x + 1, 1:10] = u.astype(BF16)
        v2[x + 1, 0, :, 128:256] = pltpu.roll(u[8, :, 128:256], 1, 0).astype(BF16)
        v2[x + 1, 10, :, 0:128] = pltpu.roll(u[0, :, 0:128], 15, 0).astype(BF16)
        if x == 0:
            v2[11] = roll_rows(v2[1], 12)
        if x == 9:
            v2[0] = roll_rows(v2[10], 4)

    weight = rise_fine[...].reshape(256, 128)
    for i in (0, 4, 1, 2, 3):
        parts = []
        for lift in range(3):
            rows = slice(2 * i + lift, 2 * i + lift + 2)
            parts.append(v2[rows, 1:10].reshape(288, 256))
            parts.append(v2[rows, 2:11, :, 0:128].reshape(288, 128))
            parts.append(v2[rows, 0:9, :, 128:256].reshape(288, 128))
        v = silu(nt(jnp.concatenate(parts, axis=1), w_dm[...])).astype(BF16)
        for b in (0, 1):
            u = nt(v[:, b * 128 : b * 128 + 128], weight).reshape(2, 9, 16, 256)
            u = u + h1[2 * i : 2 * i + 2, :, b].astype(F32)
            put_phases(f1m, f1s, 2 * i, b, u * mask2[2 * i : 2 * i + 2])
        if i == 0:
            close_below(f1m, f1s)
        if i == 4:
            close_above(f1m, f1s)

    for x in (0, 9, 1, 2, 3, 4, 5, 6, 7, 8):
        v = silu(nt(phase_window(f1m, f1s, x, 1), w_df[...])).reshape(1, 9, 2, 16, 256)
        for b in (0, 1):
            put_phases(f2m, f2s, x, b, v[:, :, b] * mask2[x : x + 1])
        if x == 0:
            close_below(f2m, f2s)
        if x == 9:
            close_above(f2m, f2s)

    parts = []
    for x in range(12):
        for low in (0, 128):
            if (x, low) not in ((0, 0), (11, 128)):
                parts.append(f2m[x, :, :, :, low : low + 128].reshape(288, 128))
                parts.append(f2s[x, 1:10, :, :, low : low + 128].reshape(288, 128))
    out = nt(jnp.concatenate(parts, axis=1), w_lv[...])

    turned[...] = out.T.reshape(16, 2, 8, 288)
    total = None
    for b in (0, 1):
        line = iota((288, 512), 0)
        lane = iota((288, 512), 1)
        block = lax.rem(line, 16)
        tgt = 36 * lax.rem(block, 4) + 2 * (line // 16) + b - 8
        spot = onehot((block // 4 == lane // 128) & (tgt == lax.rem(lane, 128)))
        term = nn(turned[0:10, b].reshape(80, 288).astype(BF16), spot)
        total = term if total is None else total + term
    for rb in range(4):
        outf[rb] = total[:, rb * 128 : rb * 128 + 128]
    for rb in range(4):
        begin, end = max(0, 4 - 10 * rb), min(10, 36 - 10 * rb)
        for a in (0, 1):
            for o in range(3):
                guess[o, pl.ds(20 * rb + 2 * begin + a - 8, end - begin, stride=2), :] = outf[
                    rb, pl.ds(8 * begin + 3 * a + o, end - begin, stride=8), :
                ]
    for c in range(3):
        clean = (noisy[0, c].astype(F32) - coef[0, 0:1] * guess[c]) / coef[1, 0:1]
        kept[c] = coef[2, 0:1] * clean

    to_mate.wait_send()
    for copy in halo:
        copy.wait_send()
    for j, k in rest:
        copy_h(j, k).wait_send()
    for k in far:
        copy_s(k).wait_send()
    for i in range(5):
        copy_x(i, 1).wait_send()
        copy_x(i, -1).wait_send()


def solution(mesh):
    sizes = tuple(mesh.shape[a] for a in ("plane", "span", "height"))
    planes, spans, heights = sizes

    def shards(*args):
        args = list(args)
        args[5] = args[5].T
        args[6] = args[6].transpose(0, 2, 1)
        args[7] = args[7].transpose(0, 2, 1)
        in_vmem = pl.BlockSpec(memory_space=pltpu.VMEM)
        in_smem = pl.BlockSpec(memory_space=pltpu.SMEM)
        in_any = pl.BlockSpec(memory_space=pl.ANY)
        vmem = pltpu.VMEM
        order = [1, 0] + list(range(4, 17))
        scratch = [vmem(args[k].shape, args[k].dtype) for k in order] + [
            vmem((2, planes // 2, 3, 32, 256), BF16),
            vmem((planes // 2, 3, 32, 256), BF16),
            vmem((planes // 2, 3, 40, 256), F32),
            vmem((48, 256), F32),
            vmem((planes // 2, heights, 5, 8, 256), BF16),
            vmem((planes // 2, heights, 5, 8, 256), BF16),
            vmem((5, 8, 256), F32),
            vmem((spans, 8, 128), BF16),
            vmem((spans, 8, 128), BF16),
            vmem((3, 3, 96, 128), BF16),
            vmem((2, 96, 128), F32),
            vmem((8, 256, 128), F32),
            vmem((2, 288, 512), F32),
            vmem((2, 288, 512), BF16),
            vmem((160, 128), F32),
            vmem((8, 640), F32),
            vmem((3, 8, 128), F32),
            vmem((256, 512), F32),
            vmem((7, 256, 512), BF16),
            vmem((256, 128), BF16),
            vmem((256, 512), BF16),
            vmem((256, 384), BF16),
            vmem((256, 1536), BF16),
            vmem((256, 1024), BF16),
            vmem((16, 1024), F32),
            vmem((256, 5632), BF16),
            vmem((5, 9, 16, 256), F32),
            vmem((10, 9, 16, 256), F32),
            vmem((10, 9, 2, 16, 256), BF16),
            vmem((10, 9, 16, 256), BF16),
            vmem((5, 9, 16, 256), BF16),
            vmem((3, 5, 9, 16, 128), BF16),
            vmem((7, 11, 16, 256), BF16),
            vmem((5, 9, 16, 256), BF16),
            vmem((12, 11, 16, 256), BF16),
            vmem((12, 9, 2, 16, 256), BF16),
            vmem((12, 11, 2, 16, 256), BF16),
            vmem((12, 9, 2, 16, 256), BF16),
            vmem((12, 11, 2, 16, 256), BF16),
            vmem((16, 2, 8, 288), F32),
            vmem((4, 80, 128), F32),
            pltpu.SemaphoreType.DMA((15,)),
            pltpu.SemaphoreType.DMA((2, 1)),
            pltpu.SemaphoreType.DMA((2, planes // 2, heights)),
            pltpu.SemaphoreType.DMA((2, spans)),
            pltpu.SemaphoreType.DMA((2, 8)),
            pltpu.SemaphoreType.DMA((2, 2, 5)),
        ]
        guess, kept, again = pl.pallas_call(
            lambda *refs: body(sizes, *refs),
            out_shape=(
                jax.ShapeDtypeStruct((3, 64, 128), F32),
                jax.ShapeDtypeStruct((3, 64, 128), F32),
                jax.ShapeDtypeStruct((64, 128), F32),
            ),
            in_specs=[in_any, in_any, in_smem, in_smem] + [in_any] * 13,
            out_specs=(in_vmem, in_vmem, in_vmem),
            scratch_shapes=scratch,
            compiler_params=pltpu.CompilerParams(
                collective_id=0, has_side_effects=True, vmem_limit_bytes=56 * 1024 * 1024
            ),
            name="denoise",
        )(*args)
        return guess[None].astype(BF16), (kept + again * guess)[None]

    in_specs = (
        P("plane", None, "height", "span"),
        P(("plane", "span", "height"), None, None, None, None),
    ) + (P(),) * 15
    out_specs = (P("plane", None, "height", "span"), P("plane", None, "height", "span"))
    return jax.shard_map(shards, mesh=mesh, in_specs=in_specs, out_specs=out_specs, check_vma=False)
```

```python
import math

import jax
import jax.numpy as jnp
from jax import lax
from jax.experimental import pallas as pl
from jax.experimental.pallas import tpu as pltpu
from jax.sharding import PartitionSpec as P

TSTEPS = 1000
STRIDE = 20
F32 = jnp.float32
BF16 = jnp.bfloat16
MESH = pl.DeviceIdType.MESH
HIGHEST = lax.Precision.HIGHEST


def nt(a, b):
    return lax.dot_general(a, b, (((1,), (1,)), ((), ())), preferred_element_type=F32)


def nn(a, b):
    return lax.dot_general(a, b, (((1,), (0,)), ((), ())), preferred_element_type=F32)


def tn(a, b):
    return lax.dot_general(a, b, (((0,), (0,)), ((), ())), preferred_element_type=F32)


def silu(v):
    return v * (0.5 * jnp.tanh(0.5 * v) + 0.5)


def iota(shape, dim):
    return lax.broadcasted_iota(jnp.int32, shape, dim)


def onehot(cond):
    return jnp.where(cond, 1.0, 0.0).astype(BF16)


def roll_rows(v, shift):
    return pltpu.roll(v.astype(F32), shift, v.ndim - 2).astype(BF16)


def plan_of(step):
    phase = (step / TSTEPS + 0.008) / 1.008 * (math.pi / 2.0)
    return jnp.cos(phase) ** 2


WINDOW = ((0, 128), (256, 512), (384, 640), (768, 896))


def phase_window(main, side, x, n):
    def flat(v):
        return v.reshape(n * 288, v.shape[-1])

    above, here, below = slice(x, x + n), slice(x + 1, x + 1 + n), slice(x + 2, x + 2 + n)
    return jnp.concatenate(
        [
            flat(main[above, :, :, :, 128:256]),
            flat(side[above, 1:10, :, :, 128:256]),
            flat(main[here]),
            flat(side[here, 1:10]),
            flat(main[below, :, :, :, 0:128]),
            flat(side[below, 1:10, :, :, 0:128]),
        ],
        axis=1,
    )


def put_phases(main, side, x, b, v):
    rows = slice(x + 1, x + 1 + v.shape[0])
    below, above = (slice(1, 10), slice(2, 11)) if b else (slice(0, 9), slice(1, 10))
    edge = pltpu.roll(v[:, 8], 1, 1) if b else pltpu.roll(v[:, 0], 15, 1)
    v, edge = v.astype(BF16), edge.astype(BF16)
    main[rows, :, b] = v
    for low in (0, 128):
        side[rows, below, 1 - b, :, low : low + 64] = v[..., low : low + 64]
        side[rows, above, 1 - b, :, low + 64 : low + 128] = v[..., low + 64 : low + 128]
    for low in (0, 128):
        if b:
            side[rows, 1, 0, :, low + 64 : low + 128] = edge[..., low + 64 : low + 128]
        else:
            side[rows, 9, 1, :, low : low + 64] = edge[..., low : low + 64]


def close_below(main, side):
    main[11, :, :, :, 0:128] = roll_rows(main[1, :, :, :, 0:128], 12)
    side[11, 1:10, :, :, 0:128] = roll_rows(side[1, 1:10, :, :, 0:128], 12)


def close_above(main, side):
    main[0, :, :, :, 128:256] = roll_rows(main[10, :, :, :, 128:256], 4)
    side[0, 1:10, :, :, 128:256] = roll_rows(side[10, 1:10, :, :, 128:256], 4)


def body(sizes, noisy_hbm, slot_hbm, timestep, owner, *refs):
    weights_hbm, outputs, local, refs = refs[:13], refs[13:16], refs[16:31], refs[31:]
    guess, kept, again = outputs
    slot, noisy, *weights = local
    (w_embed, w_biases, w_enter, pool_fine, pool_mid, w_squeeze, w_across) = weights[:7]
    (w_middle, rise_mid, decode_mid, rise_fine, decode_fine, w_leave) = weights[7:]
    (send_p, got_c, planef, heightf, send_h, got_h, rowsf, send_s, got_s, send_t, got_t) = refs[:11]
    refs = refs[11:]
    (around, aroundf, entryf, tapf, tap, condf, bias, coef, bandf, w_in, w_pf, w_pm) = refs[:12]
    (w_ac, w_dm, w_df, leavef, w_lv, mask, mask2, h1, d1, d2, sq, mx, c3, v2, e2) = refs[12:27]
    (f1m, f1s, f2m, f2s, turned, outf) = refs[27:33]
    (sem_w, sem_c, sem_h, sem_s, sem_n, sem_x) = refs[33:]
    planes, spans, heights = sizes
    p, s, h = (lax.axis_index(a) for a in ("plane", "span", "height"))

    def at(dp, ds, dh):
        return (
            lax.rem(p + (dp + planes), planes),
            lax.rem(s + (ds + spans), spans),
            lax.rem(h + (dh + heights), heights),
        )

    core = lax.rem(p, 2)
    mate = 1 - 2 * core
    chip = p // 2
    chips = planes // 2

    loads = [
        pltpu.make_async_copy(src, dst, sem_w.at[k])
        for k, (src, dst) in enumerate(zip((slot_hbm, noisy_hbm) + weights_hbm, local))
    ]
    for load in loads:
        load.start()

    barrier = pltpu.get_barrier_semaphore()
    partners = [(mate, 0, 0), (-mate, 0, 0)]
    partners += [(2 * j, 0, k) for j in range(chips) for k in range(heights) if j or k]
    seat = [lax.rem(s, 4), s // 4]
    inner = [lax.rem(seat[0] + k, 4) - seat[0] for k in range(1, 4)]
    partners += [(0, ds, 0) for ds in inner]
    partners += [(0, 4 * k, 0) for k in range(1, spans // 4)]
    partners += [(0, 1, 0), (0, -1, 0)]
    for offset in partners:
        pl.semaphore_signal(barrier, inc=1, device_id=at(*offset), device_id_type=MESH)
    def remote(src, dst, sems, index, offset):
        return pltpu.make_async_remote_copy(
            src_ref=src,
            dst_ref=dst,
            send_sem=sems.at[(0,) + index],
            recv_sem=sems.at[(1,) + index],
            device_id=at(*offset),
            device_id_type=MESH,
        )

    loads[0].wait()
    loads[1].wait()
    mine = (owner[0] == (p * spans + s) * heights + h).astype(F32)
    for k in range(planes):
        send_p[k % 2, k // 2] = (slot[0, k].astype(F32) * mine).astype(BF16)
    pl.semaphore_wait(barrier, len(partners))
    pieces = [jj for jj in (2, 1, 3, 0) if jj < chips]

    def copy_c(jj):
        src = send_p.at[1 - core, lax.rem(chip + jj, chips)]
        return remote(src, got_c.at[jj], sem_c, (jj,), (mate, 0, 0))

    for jj in pieces:
        copy_c(jj).start()

    below = remote(
        noisy.at[0, :, 48:64], around.at[1, :, 0:16], sem_n, (0,), (0, 0, 1)
    )
    above = remote(
        noisy.at[0, :, 0:16], around.at[1, :, 80:96], sem_n, (1,), (0, 0, -1)
    )
    after = remote(around.at[1], around.at[0], sem_n, (2,), (0, 1, 0))
    before = remote(around.at[1], around.at[2], sem_n, (3,), (0, -1, 0))
    below.start()
    above.start()
    around[1, :, 16:80, :] = noisy[0]

    heightf[...] = jnp.zeros_like(heightf)
    planef[...] = jnp.zeros_like(planef)

    def copy_h(jj, k):
        src = send_h.at[jj, lax.rem(h + k, heights)]
        return remote(src, got_h.at[chip, h], sem_h, (jj, k), (2 * jj, 0, k))

    rest = [(jj, k) for jj in pieces for k in (2, 1, 3, 0) if k < heights and (jj or k)]
    for jj in pieces:
        copy_c(jj).wait_recv()
        sent = send_p[core, lax.rem(chip + jj, chips)].astype(F32)
        planef[jj, :, 2:34, :] = sent + got_c[jj].astype(F32)
        for k in range(heights):
            for c in range(3):
                heightf[12 * c : 12 * c + 12, :] = planef[jj, c, 8 * k : 8 * k + 12, :]
            send_h[jj, k] = heightf[0:40, :].reshape(5, 8, 256).astype(BF16)
        for k in (2, 1, 3, 0):
            if k < heights and (jj or k):
                copy_h(jj, k).start()
    got_h[chip, h] = send_h[0, h]
    below.wait_recv()
    above.wait_recv()
    after.start()
    before.start()
    for load in loads[2:]:
        load.wait()

    now_step = jnp.full((8, 128), timestep[0].astype(F32), F32)
    now = plan_of(now_step)
    prior = plan_of(now_step - STRIDE)
    coef[0] = jnp.sqrt(1.0 - now)
    coef[1] = jnp.sqrt(now)
    coef[2] = jnp.sqrt(prior)
    again[...] = jnp.broadcast_to(jnp.sqrt(1.0 - prior)[0:1], (64, 128))
    lane = iota((8, 64), 1)
    order = jnp.where(lane < 32, lane, lane - 32).astype(F32)
    angle = timestep[0].astype(F32) * jnp.exp(order * (-math.log(10000.0) / 32))
    waves = jnp.where(lane < 32, jnp.sin(angle), jnp.cos(angle))
    hidden = jnp.dot(waves, w_embed[...], precision=HIGHEST, preferred_element_type=F32)
    hidden = hidden / (1.0 + jnp.exp(-hidden))
    flat = lax.dot_general(
        hidden, w_biases[...], (((1,), (1,)), ((), ())), HIGHEST, preferred_element_type=F32
    )
    col = iota((448, 640), 1)
    pick = jnp.where(col < 256, lax.rem(col, 64), col - 192)
    pick = jnp.where(iota((448, 640), 0) == pick, 1.0, 0.0)
    bias[...] = jnp.dot(flat, pick, precision=HIGHEST, preferred_element_type=F32)

    w_df[...] = jnp.zeros_like(w_df)
    w_lv[...] = jnp.zeros_like(w_lv)
    leavef[...] = jnp.zeros_like(leavef)
    for b in (0, 1):
        place = iota((192, 256), 1)
        tapcol = lax.rem(place // 64 + 1, 4) - b
        spot = onehot(
            (tapcol >= 0)
            & (tapcol <= 2)
            & (iota((192, 256), 0) == tapcol * 64 + lax.rem(place, 64))
        )
        for lift in range(3):
            block = nn(decode_fine[lift], spot).astype(BF16)
            final = nn(w_leave[lift], spot)
            for a in (0, 1):
                first, second = WINDOW[a + lift]
                rows = slice(a * 128 + b * 64, a * 128 + b * 64 + 64)
                w_df[rows, first : first + 128] = block[:, 0:128]
                w_df[rows, second : second + 128] = block[:, 128:256]
                rows = slice(b * 8 + a * 3, b * 8 + a * 3 + 3)
                leavef[rows, first : first + 128] = final[:, 0:128]
                leavef[rows, second : second + 128] = final[:, 128:256]
    final = leavef[...].astype(BF16)
    for x in range(10):
        for k, begin in enumerate((0, 128, 256, 512, 384, 640, 768, 896)):
            spot = 512 * x + 128 * k
            w_lv[16 * x : 16 * x + 16, spot : spot + 128] = final[:, begin : begin + 128]

    for k in range(4):
        w_pf[k * 64 : k * 64 + 64, :] = pool_fine[k]
        w_pm[:, k * 128 : k * 128 + 128] = pool_mid[k]
    has_before = (p > 0).astype(F32)
    has_after = (p < planes - 1).astype(F32)
    w_ac[:, 0:128] = (w_across[0].astype(F32) * has_before).astype(BF16)
    w_ac[:, 128:256] = w_across[1]
    w_ac[:, 256:384] = (w_across[2].astype(F32) * has_after).astype(BF16)
    w_dm[...] = jnp.zeros_like(w_dm)
    for b in (0, 1):
        for lift in range(3):
            for step in range(3):
                spot = 512 * lift + 128 * ((b + step + 3) % 4)
                w_dm[b * 128 : b * 128 + 128, spot : spot + 128] = decode_mid[
                    lift, :, step * 128 : step * 128 + 128
                ]

    for a in (0, 1):
        for b in (0, 1):
            total = None
            for lift in range(3):
                k = iota((18, 512), 0)
                tgt = (k // 6 + b) * 128 + (a + lift) * 8 + lax.rem(k, 6)
                term = tn(w_enter[lift], onehot(iota((18, 512), 1) == tgt))
                total = term if total is None else total + term
            bandf[a * 128 + b * 64 : a * 128 + b * 64 + 64, :] = total
    for x in range(7):
        for wc in range(4):
            lanes = slice(wc * 128, wc * 128 + 128)
            v = bandf[:, lanes]
            w_in[x, :, lanes] = (v if x == 0 else pltpu.roll(v, 16 * x, 1)).astype(BF16)

    shape = (5, 9, 16, 256)
    block = iota(shape, 2)
    row = (block // 4) * 5 + iota(shape, 0) - 2
    col = lax.rem(block, 4) * 9 + iota(shape, 1) - 2
    low_row, high_row = jnp.where(h == 0, 0, -9), jnp.where(h == heights - 1, 16, 99)
    low_col, high_col = jnp.where(s == 0, 0, -9), jnp.where(s == spans - 1, 32, 99)
    inside = (row >= low_row) & (row < high_row) & (col >= low_col) & (col < high_col)
    mask[...] = jnp.where(inside, 1.0, 0.0)
    for x in range(10):
        mask2[x] = mask[x // 2]

    after.wait_recv()
    before.wait_recv()
    row = iota((96, 128), 0)
    rows_in = jnp.where((row >= jnp.where(h == 0, 16, 0)) & (row < jnp.where(h == heights - 1, 80, 96)), 1.0, 0.0)
    right = rows_in * (s < spans - 1).astype(F32)
    left = rows_in * (s > 0).astype(F32)
    near = iota((96, 128), 1) < 64
    entryf[...] = jnp.zeros_like(entryf)
    for c in range(3):
        aroundf[0] = around[1, c].astype(F32) * rows_in
        aroundf[1] = jnp.where(
            near, around[2, c].astype(F32) * right, around[0, c].astype(F32) * left
        )
        for rb in range(4):
            for part in range(2):
                entryf[2 * rb + part, pl.ds(c, 22, stride=8), :] = aroundf[
                    part, 7 + 20 * rb : 29 + 20 * rb, :
                ]
    entry = jnp.concatenate([entryf[k] for k in range(8)], axis=1).astype(BF16)
    line = iota((288, 1), 0)
    block = lax.rem(line, 16)
    cell = 36 * lax.rem(block, 4) + 2 * (line // 16) - 9
    for wc in range(4):
        tgt = (block // 4) * 256 + ((cell + wc) & 255)
        spot = onehot(iota((288, 1024), 1) == tgt)
        for g in range(2):
            tapf[g, :, wc * 128 : wc * 128 + 128] = nt(spot, entry[48 * g : 48 * g + 128])

    for j, k in rest:
        copy_h(j, k).wait_recv()
    total = None
    for j in range(chips):
        for k in range(heights):
            term = got_h[j, k].astype(F32)
            total = term if total is None else total + term
    rowsf[...] = total

    lane = iota((8, 128), 1)
    for dest in range(spans):
        total = jnp.zeros((8, 128), F32)
        for g in range(5):
            shift = (24 * g + 2 - 16 * dest) % 256
            v = rowsf[g]
            moved = (pltpu.roll(v, shift, 1) if shift else v)[:, 0:128]
            total = jnp.where((lane >= 24 * g) & (lane < 24 * g + 20), moved, total)
        send_s[dest % 4, dest // 4] = total.astype(BF16)

    spot_in, four = seat

    def copy_s(k):
        src = send_s.at[lax.rem(spot_in + k, 4)]
        return remote(src, got_s.at[spot_in], sem_s, (0, k), (0, inner[k - 1], 0))

    def copy_t(k):
        src = send_t.at[lax.rem(four + k, spans // 4)]
        return remote(src, got_t.at[four], sem_s, (1, k), (0, 4 * k, 0))

    for k in range(1, 4):
        copy_s(k).start()
    got_s[spot_in] = send_s[spot_in]
    for k in range(1, 4):
        copy_s(k).wait_recv()
    total = got_s[0].astype(F32)
    for k in range(1, 4):
        total = total + got_s[k].astype(F32)
    send_t[...] = total.astype(BF16)
    for k in range(1, spans // 4):
        copy_t(k).start()
    got_t[four] = send_t[four]
    for k in range(1, spans // 4):
        copy_t(k).wait_recv()
    total = got_t[0].astype(F32)
    for k in range(1, spans // 4):
        total = total + got_t[k].astype(F32)
    lane = iota((8, 128), 1)
    spot = lane - 24 * (lane // 24)
    outside = ((spot < 2) & (s == 0)) | ((spot >= 18) & (s == spans - 1))
    total = jnp.where(outside, 0.0, total)
    for g in range(5):
        part = total if g == 0 else pltpu.roll(total, 128 - 24 * g, 1)
        part = jnp.where(lane < 20, part, 0.0)
        for rb in range(4):
            condf[rb * 40 + 8 * g : rb * 40 + 8 * g + 8, :] = (
                part if rb == 0 else pltpu.roll(part, 32 * rb, 1)
            )
    line = iota((256, 160), 0)
    channel = lax.rem(line, 8) - 3
    m = iota((256, 160), 1)
    rb = m // 40
    tgt = channel * 12 + (rb * 20 + line // 8 + 7) // 8
    pick = (channel >= 0) & (channel < 3) & (line < 176) & (m - 40 * rb == tgt)
    lifted = nn(onehot(pick), condf[...].astype(BF16)).astype(BF16)
    line = iota((288, 1), 0)
    block = lax.rem(line, 16)
    cell = 36 * lax.rem(block, 4) + 2 * (line // 16) - 9
    for wc in range(4):
        tgt = (block // 4) * 32 + (cell + wc + 16) // 8
        spot = onehot(iota((288, 128), 1) == tgt)
        lanes = slice(wc * 128, wc * 128 + 128)
        for g in range(2):
            v = tapf[g, :, lanes] + nt(spot, lifted[48 * g : 48 * g + 128])
            tap[g, :, lanes] = v.astype(BF16)

    groups = ((0, 1, 2), (3, 4))

    def copy_x(g, way):
        rows = slice(groups[g][0], groups[g][-1] + 1)
        side = 0 if way == 1 else 2
        return remote(
            sq.at[1, rows], sq.at[side, rows], sem_x, (0 if way == 1 else 1, g), (way, 0, 0)
        )

    for x in range(10):
        v = nt(tap[x // 5], w_in[x - 3 * (x // 5)])
        h1[x] = silu(v + bias[0:1, 0:256]).astype(BF16).reshape(9, 2, 16, 256)
    for g, group in enumerate(groups):
        for x in range(2 * group[0], 2 * group[-1] + 2):
            v = nn(h1[x].reshape(288, 256), w_pf[...]) + bias[0:1, 256:384]
            v = silu(v).astype(BF16).reshape(9, 2, 16, 128)
            d1[x, :, :, 0:128] = v[:, 0]
            d1[x, :, :, 128:256] = v[:, 1]
        n = 144 * len(group)
        rows = slice(group[0], group[-1] + 1)
        parts = [
            jnp.concatenate([d1[2 * i + a].reshape(144, 256) for i in group], axis=0)
            for a in (0, 1)
        ]
        v = silu(nt(jnp.concatenate(parts, axis=1), w_pm[...]) + bias[0:1, 384:640]).astype(BF16)
        d2[rows] = v.reshape(len(group), 9, 16, 256)
        v = nt(v, w_squeeze[...]).astype(BF16)
        sq[1, rows] = v.reshape(len(group), 9, 16, 128)
        copy_x(g, 1).start()
        copy_x(g, -1).start()

    for i in range(5):
        if i in (0, 3):
            copy_x(i // 3, 1).wait_recv()
            copy_x(i // 3, -1).wait_recv()
        v = jnp.concatenate([sq[t, i].reshape(144, 128) for t in range(3)], axis=1)
        v = nt(v, w_ac[...]).reshape(9, 16, 256) + d2[i].astype(F32)
        v = v * mask[i]
        mx[i + 1, 1:10] = v.astype(BF16)
        mx[i + 1, 0] = pltpu.roll(v[8], 1, 0).astype(BF16)
        mx[i + 1, 10] = pltpu.roll(v[0], 15, 0).astype(BF16)
        if i == 0:
            mx[6] = roll_rows(mx[1], 12)
        if i == 4:
            mx[0] = roll_rows(mx[5], 4)

    total = None
    for lift in range(3):
        v = jnp.concatenate(
            [mx[lift : lift + 5, step : step + 9].reshape(720, 256) for step in range(3)], axis=1
        )
        term = nt(v, w_middle[lift])
        total = term if total is None else total + term
    c3[...] = silu(total).astype(BF16).reshape(5, 9, 16, 256)

    v = nt(c3[...].reshape(720, 256), rise_mid[...].reshape(512, 256)).reshape(5, 9, 16, 512)
    for x in (0, 9, 1, 2, 3, 4, 5, 6, 7, 8):
        u = v[x // 2, :, :, x % 2 * 256 : x % 2 * 256 + 256] + d1[x].astype(F32)
        u = u * mask2[x]
        v2[x + 1, 1:10] = u.astype(BF16)
        v2[x + 1, 0, :, 128:256] = pltpu.roll(u[8, :, 128:256], 1, 0).astype(BF16)
        v2[x + 1, 10, :, 0:128] = pltpu.roll(u[0, :, 0:128], 15, 0).astype(BF16)
        if x == 0:
            v2[11] = roll_rows(v2[1], 12)
        if x == 9:
            v2[0] = roll_rows(v2[10], 4)

    weight = rise_fine[...].reshape(256, 128)
    for i in (0, 4, 1, 2, 3):
        parts = []
        for lift in range(3):
            rows = slice(2 * i + lift, 2 * i + lift + 2)
            parts.append(v2[rows, 1:10].reshape(288, 256))
            parts.append(v2[rows, 2:11, :, 0:128].reshape(288, 128))
            parts.append(v2[rows, 0:9, :, 128:256].reshape(288, 128))
        v = silu(nt(jnp.concatenate(parts, axis=1), w_dm[...])).astype(BF16)
        e2[2 * i : 2 * i + 2] = v.reshape(2, 9, 16, 256)
    for i in (0, 4, 1, 2, 3):
        for b in (0, 1):
            v = e2[2 * i : 2 * i + 2, :, :, b * 128 : b * 128 + 128].reshape(288, 128)
            u = nt(v, weight).reshape(2, 9, 16, 256)
            u = u + h1[2 * i : 2 * i + 2, :, b].astype(F32)
            put_phases(f1m, f1s, 2 * i, b, u * mask2[2 * i : 2 * i + 2])
        if i == 0:
            close_below(f1m, f1s)
        if i == 4:
            close_above(f1m, f1s)

    for x in (0, 9, 1, 2, 3, 4, 5, 6, 7, 8):
        v = silu(nt(phase_window(f1m, f1s, x, 1), w_df[...])).reshape(1, 9, 2, 16, 256)
        for b in (0, 1):
            put_phases(f2m, f2s, x, b, v[:, :, b] * mask2[x : x + 1])
        if x == 0:
            close_below(f2m, f2s)
        if x == 9:
            close_above(f2m, f2s)

    parts = []
    for x in range(12):
        for low in (0, 128):
            if (x, low) not in ((0, 0), (11, 128)):
                parts.append(f2m[x, :, :, :, low : low + 128].reshape(288, 128))
                parts.append(f2s[x, 1:10, :, :, low : low + 128].reshape(288, 128))
    out = nt(jnp.concatenate(parts, axis=1), w_lv[...])

    turned[...] = out.T.reshape(16, 2, 8, 288)
    total = None
    for b in (0, 1):
        line = iota((288, 512), 0)
        lane = iota((288, 512), 1)
        block = lax.rem(line, 16)
        tgt = 36 * lax.rem(block, 4) + 2 * (line // 16) + b - 8
        spot = onehot((block // 4 == lane // 128) & (tgt == lax.rem(lane, 128)))
        term = nn(turned[0:10, b].reshape(80, 288).astype(BF16), spot)
        total = term if total is None else total + term
    for rb in range(4):
        outf[rb] = total[:, rb * 128 : rb * 128 + 128]
    for rb in range(4):
        begin, end = max(0, 4 - 10 * rb), min(10, 36 - 10 * rb)
        for a in (0, 1):
            for o in range(3):
                guess[o, pl.ds(20 * rb + 2 * begin + a - 8, end - begin, stride=2), :] = outf[
                    rb, pl.ds(8 * begin + 3 * a + o, end - begin, stride=8), :
                ]
    for c in range(3):
        clean = (noisy[0, c].astype(F32) - coef[0, 0:1] * guess[c]) / coef[1, 0:1]
        kept[c] = coef[2, 0:1] * clean

    for jj in pieces:
        copy_c(jj).wait_send()
    for copy in (below, above, after, before):
        copy.wait_send()
    for j, k in rest:
        copy_h(j, k).wait_send()
    for k in range(1, 4):
        copy_s(k).wait_send()
    for k in range(1, spans // 4):
        copy_t(k).wait_send()
    for g in range(2):
        copy_x(g, 1).wait_send()
        copy_x(g, -1).wait_send()


def solution(mesh):
    sizes = tuple(mesh.shape[a] for a in ("plane", "span", "height"))
    planes, spans, heights = sizes

    def shards(*args):
        args = list(args)
        args[5] = args[5].T
        args[6] = args[6].transpose(0, 2, 1)
        args[7] = args[7].transpose(0, 2, 1)
        in_vmem = pl.BlockSpec(memory_space=pltpu.VMEM)
        in_smem = pl.BlockSpec(memory_space=pltpu.SMEM)
        in_any = pl.BlockSpec(memory_space=pl.ANY)
        vmem = pltpu.VMEM
        order = [1, 0] + list(range(4, 17))
        scratch = [vmem(args[k].shape, args[k].dtype) for k in order] + [
            vmem((2, planes // 2, 3, 32, 256), BF16),
            vmem((planes // 2, 3, 32, 256), BF16),
            vmem((planes // 2, 3, 40, 256), F32),
            vmem((48, 256), F32),
            vmem((planes // 2, heights, 5, 8, 256), BF16),
            vmem((planes // 2, heights, 5, 8, 256), BF16),
            vmem((5, 8, 256), F32),
            vmem((4, spans // 4, 8, 128), BF16),
            vmem((4, spans // 4, 8, 128), BF16),
            vmem((spans // 4, 8, 128), BF16),
            vmem((spans // 4, 8, 128), BF16),
            vmem((3, 3, 96, 128), BF16),
            vmem((2, 96, 128), F32),
            vmem((8, 256, 128), F32),
            vmem((2, 288, 512), F32),
            vmem((2, 288, 512), BF16),
            vmem((160, 128), F32),
            vmem((8, 640), F32),
            vmem((3, 8, 128), F32),
            vmem((256, 512), F32),
            vmem((7, 256, 512), BF16),
            vmem((256, 128), BF16),
            vmem((256, 512), BF16),
            vmem((256, 384), BF16),
            vmem((256, 1536), BF16),
            vmem((256, 1024), BF16),
            vmem((16, 1024), F32),
            vmem((256, 5632), BF16),
            vmem((5, 9, 16, 256), F32),
            vmem((10, 9, 16, 256), F32),
            vmem((10, 9, 2, 16, 256), BF16),
            vmem((10, 9, 16, 256), BF16),
            vmem((5, 9, 16, 256), BF16),
            vmem((3, 5, 9, 16, 128), BF16),
            vmem((7, 11, 16, 256), BF16),
            vmem((5, 9, 16, 256), BF16),
            vmem((12, 11, 16, 256), BF16),
            vmem((10, 9, 16, 256), BF16),
            vmem((12, 9, 2, 16, 256), BF16),
            vmem((12, 11, 2, 16, 256), BF16),
            vmem((12, 9, 2, 16, 256), BF16),
            vmem((12, 11, 2, 16, 256), BF16),
            vmem((16, 2, 8, 288), F32),
            vmem((4, 80, 128), F32),
            pltpu.SemaphoreType.DMA((15,)),
            pltpu.SemaphoreType.DMA((2, planes // 2)),
            pltpu.SemaphoreType.DMA((2, planes // 2, heights)),
            pltpu.SemaphoreType.DMA((2, 2, 4)),
            pltpu.SemaphoreType.DMA((2, 4)),
            pltpu.SemaphoreType.DMA((2, 2, 2)),
        ]
        guess, kept, again = pl.pallas_call(
            lambda *refs: body(sizes, *refs),
            out_shape=(
                jax.ShapeDtypeStruct((3, 64, 128), F32),
                jax.ShapeDtypeStruct((3, 64, 128), F32),
                jax.ShapeDtypeStruct((64, 128), F32),
            ),
            in_specs=[in_any, in_any, in_smem, in_smem] + [in_any] * 13,
            out_specs=(in_vmem, in_vmem, in_vmem),
            scratch_shapes=scratch,
            compiler_params=pltpu.CompilerParams(
                collective_id=0, has_side_effects=True, vmem_limit_bytes=56 * 1024 * 1024
            ),
            name="denoise",
        )(*args)
        return guess[None].astype(BF16), (kept + again * guess)[None]

    in_specs = (
        P("plane", None, "height", "span"),
        P(("plane", "span", "height"), None, None, None, None),
    ) + (P(),) * 15
    out_specs = (P("plane", None, "height", "span"), P("plane", None, "height", "span"))
    return jax.shard_map(shards, mesh=mesh, in_specs=in_specs, out_specs=out_specs, check_vma=False)
```

```python
import math

import jax
import jax.numpy as jnp
from jax import lax
from jax.experimental import pallas as pl
from jax.experimental.pallas import tpu as pltpu
from jax.sharding import PartitionSpec as P

TSTEPS = 1000
STRIDE = 20
F32 = jnp.float32
BF16 = jnp.bfloat16
MESH = pl.DeviceIdType.MESH
HIGHEST = lax.Precision.HIGHEST


def nt(a, b):
    return lax.dot_general(a, b, (((1,), (1,)), ((), ())), preferred_element_type=F32)


def nn(a, b):
    return lax.dot_general(a, b, (((1,), (0,)), ((), ())), preferred_element_type=F32)


def tn(a, b):
    return lax.dot_general(a, b, (((0,), (0,)), ((), ())), preferred_element_type=F32)


def silu(v):
    return v * (0.5 * jnp.tanh(0.5 * v) + 0.5)


def iota(shape, dim):
    return lax.broadcasted_iota(jnp.int32, shape, dim)


def onehot(cond):
    return jnp.where(cond, 1.0, 0.0).astype(BF16)


def roll_rows(v, shift):
    return pltpu.roll(v.astype(F32), shift, v.ndim - 2).astype(BF16)


def plan_of(step):
    phase = (step / TSTEPS + 0.008) / 1.008 * (math.pi / 2.0)
    return jnp.cos(phase) ** 2


WINDOW = ((0, 128), (256, 512), (384, 640), (768, 896))


def phase_window(main, side, x, n):
    def flat(v):
        return v.reshape(n * 288, v.shape[-1])

    above, here, below = slice(x, x + n), slice(x + 1, x + 1 + n), slice(x + 2, x + 2 + n)
    return jnp.concatenate(
        [
            flat(main[above, :, :, :, 128:256]),
            flat(side[above, 1:10, :, :, 128:256]),
            flat(main[here]),
            flat(side[here, 1:10]),
            flat(main[below, :, :, :, 0:128]),
            flat(side[below, 1:10, :, :, 0:128]),
        ],
        axis=1,
    )


def put_phases(main, side, x, b, v):
    rows = slice(x + 1, x + 1 + v.shape[0])
    below, above = (slice(1, 10), slice(2, 11)) if b else (slice(0, 9), slice(1, 10))
    edge = pltpu.roll(v[:, 8], 1, 1) if b else pltpu.roll(v[:, 0], 15, 1)
    v, edge = v.astype(BF16), edge.astype(BF16)
    main[rows, :, b] = v
    for low in (0, 128):
        side[rows, below, 1 - b, :, low : low + 64] = v[..., low : low + 64]
        side[rows, above, 1 - b, :, low + 64 : low + 128] = v[..., low + 64 : low + 128]
    for low in (0, 128):
        if b:
            side[rows, 1, 0, :, low + 64 : low + 128] = edge[..., low + 64 : low + 128]
        else:
            side[rows, 9, 1, :, low : low + 64] = edge[..., low : low + 64]


def close_below(main, side):
    main[11, :, :, :, 0:128] = roll_rows(main[1, :, :, :, 0:128], 12)
    side[11, 1:10, :, :, 0:128] = roll_rows(side[1, 1:10, :, :, 0:128], 12)


def close_above(main, side):
    main[0, :, :, :, 128:256] = roll_rows(main[10, :, :, :, 128:256], 4)
    side[0, 1:10, :, :, 128:256] = roll_rows(side[10, 1:10, :, :, 128:256], 4)


def body(sizes, noisy_hbm, slot_hbm, timestep, owner, *refs):
    weights_hbm, outputs, local, refs = refs[:13], refs[13:16], refs[16:31], refs[31:]
    guess, kept, again = outputs
    slot, noisy, *weights = local
    (w_embed, w_biases, w_enter, pool_fine, pool_mid, w_squeeze, w_across) = weights[:7]
    (w_middle, rise_mid, decode_mid, rise_fine, decode_fine, w_leave) = weights[7:]
    (send_p, got_c, planef, heightf, send_h, got_h, rowsf, send_s, got_s) = refs[:9]
    refs = refs[9:]
    (around, aroundf, entryf, tapf, tap, condf, bias, coef, bandf, w_in, w_pf, w_pm) = refs[:12]
    (w_ac, w_dm, w_df, leavef, w_lv, mask, mask2, h1, d1, d2, sq, mx, c3, v2, e2) = refs[12:27]
    (f1m, f1s, f2m, f2s, turned, outf) = refs[27:33]
    (sem_w, sem_c, sem_h, sem_s, sem_n, sem_x) = refs[33:]
    planes, spans, heights = sizes
    p, s, h = (lax.axis_index(a) for a in ("plane", "span", "height"))

    def at(dp, ds, dh):
        return (
            lax.rem(p + (dp + planes), planes),
            lax.rem(s + (ds + spans), spans),
            lax.rem(h + (dh + heights), heights),
        )

    core = lax.rem(p, 2)
    mate = 1 - 2 * core
    chip = p // 2
    chips = planes // 2

    loads = [
        pltpu.make_async_copy(src, dst, sem_w.at[k])
        for k, (src, dst) in enumerate(zip((slot_hbm, noisy_hbm) + weights_hbm, local))
    ]
    for load in loads:
        load.start()

    barrier = pltpu.get_barrier_semaphore()
    partners = [(mate, 0, 0), (-mate, 0, 0)]
    partners += [(2 * j, 0, k) for j in range(chips) for k in range(heights) if j or k]
    partners += [(0, k, 0) for k in range(1, spans)]
    for offset in partners:
        pl.semaphore_signal(barrier, inc=1, device_id=at(*offset), device_id_type=MESH)
    def remote(src, dst, sems, index, offset):
        return pltpu.make_async_remote_copy(
            src_ref=src,
            dst_ref=dst,
            send_sem=sems.at[(0,) + index],
            recv_sem=sems.at[(1,) + index],
            device_id=at(*offset),
            device_id_type=MESH,
        )

    loads[0].wait()
    loads[1].wait()
    mine = (owner[0] == (p * spans + s) * heights + h).astype(F32)
    for k in range(planes):
        send_p[k % 2, k // 2] = (slot[0, k].astype(F32) * mine).astype(BF16)
    pl.semaphore_wait(barrier, len(partners))
    pieces = [jj for jj in (2, 1, 3, 0) if jj < chips]

    def copy_c(jj):
        src = send_p.at[1 - core, lax.rem(chip + jj, chips)]
        return remote(src, got_c.at[jj], sem_c, (jj,), (mate, 0, 0))

    for jj in pieces:
        copy_c(jj).start()

    below = remote(
        noisy.at[0, :, 48:64], around.at[1, :, 0:16], sem_n, (0,), (0, 0, 1)
    )
    above = remote(
        noisy.at[0, :, 0:16], around.at[1, :, 80:96], sem_n, (1,), (0, 0, -1)
    )
    after = remote(around.at[1], around.at[0], sem_n, (2,), (0, 1, 0))
    before = remote(around.at[1], around.at[2], sem_n, (3,), (0, -1, 0))
    below.start()
    above.start()
    around[1, :, 16:80, :] = noisy[0]

    heightf[...] = jnp.zeros_like(heightf)
    planef[...] = jnp.zeros_like(planef)

    def copy_h(jj, k):
        src = send_h.at[jj, lax.rem(h + k, heights)]
        return remote(src, got_h.at[chip, h], sem_h, (jj, k), (2 * jj, 0, k))

    rest = [(jj, k) for jj in pieces for k in (2, 1, 3, 0) if k < heights and (jj or k)]
    for jj in pieces:
        copy_c(jj).wait_recv()
        sent = send_p[core, lax.rem(chip + jj, chips)].astype(F32)
        planef[jj, :, 2:34, :] = sent + got_c[jj].astype(F32)
        for k in range(heights):
            for c in range(3):
                heightf[12 * c : 12 * c + 12, :] = planef[jj, c, 8 * k : 8 * k + 12, :]
            send_h[jj, k] = heightf[0:40, :].reshape(5, 8, 256).astype(BF16)
        for k in (2, 1, 3, 0):
            if k < heights and (jj or k):
                copy_h(jj, k).start()
    got_h[chip, h] = send_h[0, h]
    below.wait_recv()
    above.wait_recv()
    after.start()
    before.start()
    for load in loads[2:]:
        load.wait()

    now_step = jnp.full((8, 128), timestep[0].astype(F32), F32)
    now = plan_of(now_step)
    prior = plan_of(now_step - STRIDE)
    coef[0] = jnp.sqrt(1.0 - now)
    coef[1] = jnp.sqrt(now)
    coef[2] = jnp.sqrt(prior)
    again[...] = jnp.broadcast_to(jnp.sqrt(1.0 - prior)[0:1], (64, 128))
    lane = iota((8, 64), 1)
    order = jnp.where(lane < 32, lane, lane - 32).astype(F32)
    angle = timestep[0].astype(F32) * jnp.exp(order * (-math.log(10000.0) / 32))
    waves = jnp.where(lane < 32, jnp.sin(angle), jnp.cos(angle))
    hidden = jnp.dot(waves, w_embed[...], precision=HIGHEST, preferred_element_type=F32)
    hidden = hidden / (1.0 + jnp.exp(-hidden))
    flat = lax.dot_general(
        hidden, w_biases[...], (((1,), (1,)), ((), ())), HIGHEST, preferred_element_type=F32
    )
    col = iota((448, 640), 1)
    pick = jnp.where(col < 256, lax.rem(col, 64), col - 192)
    pick = jnp.where(iota((448, 640), 0) == pick, 1.0, 0.0)
    bias[...] = jnp.dot(flat, pick, precision=HIGHEST, preferred_element_type=F32)

    w_df[...] = jnp.zeros_like(w_df)
    w_lv[...] = jnp.zeros_like(w_lv)
    leavef[...] = jnp.zeros_like(leavef)
    for b in (0, 1):
        place = iota((192, 256), 1)
        tapcol = lax.rem(place // 64 + 1, 4) - b
        spot = onehot(
            (tapcol >= 0)
            & (tapcol <= 2)
            & (iota((192, 256), 0) == tapcol * 64 + lax.rem(place, 64))
        )
        for lift in range(3):
            block = nn(decode_fine[lift], spot).astype(BF16)
            final = nn(w_leave[lift], spot)
            for a in (0, 1):
                first, second = WINDOW[a + lift]
                rows = slice(a * 128 + b * 64, a * 128 + b * 64 + 64)
                w_df[rows, first : first + 128] = block[:, 0:128]
                w_df[rows, second : second + 128] = block[:, 128:256]
                rows = slice(b * 8 + a * 3, b * 8 + a * 3 + 3)
                leavef[rows, first : first + 128] = final[:, 0:128]
                leavef[rows, second : second + 128] = final[:, 128:256]
    final = leavef[...].astype(BF16)
    for x in range(10):
        for k, begin in enumerate((0, 128, 256, 512, 384, 640, 768, 896)):
            spot = 512 * x + 128 * k
            w_lv[16 * x : 16 * x + 16, spot : spot + 128] = final[:, begin : begin + 128]

    for k in range(4):
        w_pf[k * 64 : k * 64 + 64, :] = pool_fine[k]
        w_pm[:, k * 128 : k * 128 + 128] = pool_mid[k]
    has_before = (p > 0).astype(F32)
    has_after = (p < planes - 1).astype(F32)
    w_ac[:, 0:128] = (w_across[0].astype(F32) * has_before).astype(BF16)
    w_ac[:, 128:256] = w_across[1]
    w_ac[:, 256:384] = (w_across[2].astype(F32) * has_after).astype(BF16)
    w_dm[...] = jnp.zeros_like(w_dm)
    for b in (0, 1):
        for lift in range(3):
            for step in range(3):
                spot = 512 * lift + 128 * ((b + step + 3) % 4)
                w_dm[b * 128 : b * 128 + 128, spot : spot + 128] = decode_mid[
                    lift, :, step * 128 : step * 128 + 128
                ]

    for a in (0, 1):
        for b in (0, 1):
            total = None
            for lift in range(3):
                k = iota((18, 512), 0)
                tgt = (k // 6 + b) * 128 + (a + lift) * 8 + lax.rem(k, 6)
                term = tn(w_enter[lift], onehot(iota((18, 512), 1) == tgt))
                total = term if total is None else total + term
            bandf[a * 128 + b * 64 : a * 128 + b * 64 + 64, :] = total
    for x in range(7):
        for wc in range(4):
            lanes = slice(wc * 128, wc * 128 + 128)
            v = bandf[:, lanes]
            w_in[x, :, lanes] = (v if x == 0 else pltpu.roll(v, 16 * x, 1)).astype(BF16)

    shape = (5, 9, 16, 256)
    block = iota(shape, 2)
    row = (block // 4) * 5 + iota(shape, 0) - 2
    col = lax.rem(block, 4) * 9 + iota(shape, 1) - 2
    low_row, high_row = jnp.where(h == 0, 0, -9), jnp.where(h == heights - 1, 16, 99)
    low_col, high_col = jnp.where(s == 0, 0, -9), jnp.where(s == spans - 1, 32, 99)
    inside = (row >= low_row) & (row < high_row) & (col >= low_col) & (col < high_col)
    mask[...] = jnp.where(inside, 1.0, 0.0)
    for x in range(10):
        mask2[x] = mask[x // 2]

    after.wait_recv()
    before.wait_recv()
    row = iota((96, 128), 0)
    rows_in = jnp.where((row >= jnp.where(h == 0, 16, 0)) & (row < jnp.where(h == heights - 1, 80, 96)), 1.0, 0.0)
    right = rows_in * (s < spans - 1).astype(F32)
    left = rows_in * (s > 0).astype(F32)
    near = iota((96, 128), 1) < 64
    entryf[...] = jnp.zeros_like(entryf)
    for c in range(3):
        aroundf[0] = around[1, c].astype(F32) * rows_in
        aroundf[1] = jnp.where(
            near, around[2, c].astype(F32) * right, around[0, c].astype(F32) * left
        )
        for rb in range(4):
            for part in range(2):
                entryf[2 * rb + part, pl.ds(c, 22, stride=8), :] = aroundf[
                    part, 7 + 20 * rb : 29 + 20 * rb, :
                ]
    entry = jnp.concatenate([entryf[k] for k in range(8)], axis=1).astype(BF16)
    line = iota((288, 1), 0)
    block = lax.rem(line, 16)
    cell = 36 * lax.rem(block, 4) + 2 * (line // 16) - 9
    for wc in range(4):
        tgt = (block // 4) * 256 + ((cell + wc) & 255)
        spot = onehot(iota((288, 1024), 1) == tgt)
        for g in range(2):
            tapf[g, :, wc * 128 : wc * 128 + 128] = nt(spot, entry[48 * g : 48 * g + 128])

    for j, k in rest:
        copy_h(j, k).wait_recv()
    total = None
    for j in range(chips):
        for k in range(heights):
            term = got_h[j, k].astype(F32)
            total = term if total is None else total + term
    rowsf[...] = total

    moved = [rowsf[0]] + [pltpu.roll(rowsf[g], 24 * g, 1) for g in range(1, 5)]
    for dest in range(spans):
        rel = (iota((8, 256), 1) - (16 * dest - 2)) & 255
        total = moved[0]
        for g in range(1, 5):
            total = jnp.where(rel >= 24 * g, moved[g], total)
        total = pltpu.roll(total, (2 - 16 * dest) % 256, 1)[:, 0:128]
        send_s[dest] = total.astype(BF16)

    def copy_s(k):
        return remote(send_s.at[lax.rem(s + k, spans)], got_s.at[s], sem_s, (k,), (0, k, 0))

    far = sorted(range(1, spans), key=lambda k: -min(k, spans - k))
    for k in far:
        copy_s(k).start()
    got_s[s] = send_s[s]
    for k in reversed(far):
        copy_s(k).wait_recv()
    total = got_s[0].astype(F32)
    for k in range(1, spans):
        total = total + got_s[k].astype(F32)
    lane = iota((8, 128), 1)
    spot = lane - 24 * (lane // 24)
    outside = ((spot < 2) & (s == 0)) | ((spot >= 18) & (s == spans - 1))
    total = jnp.where(outside, 0.0, total)
    for g in range(5):
        part = total if g == 0 else pltpu.roll(total, 128 - 24 * g, 1)
        part = jnp.where(lane < 20, part, 0.0)
        for rb in range(4):
            condf[rb * 40 + 8 * g : rb * 40 + 8 * g + 8, :] = (
                part if rb == 0 else pltpu.roll(part, 32 * rb, 1)
            )
    line = iota((256, 160), 0)
    channel = lax.rem(line, 8) - 3
    m = iota((256, 160), 1)
    rb = m // 40
    tgt = channel * 12 + (rb * 20 + line // 8 + 7) // 8
    pick = (channel >= 0) & (channel < 3) & (line < 176) & (m - 40 * rb == tgt)
    lifted = nn(onehot(pick), condf[...].astype(BF16)).astype(BF16)
    line = iota((288, 1), 0)
    block = lax.rem(line, 16)
    cell = 36 * lax.rem(block, 4) + 2 * (line // 16) - 9
    for wc in range(4):
        tgt = (block // 4) * 32 + (cell + wc + 16) // 8
        spot = onehot(iota((288, 128), 1) == tgt)
        lanes = slice(wc * 128, wc * 128 + 128)
        for g in range(2):
            v = tapf[g, :, lanes] + nt(spot, lifted[48 * g : 48 * g + 128])
            tap[g, :, lanes] = v.astype(BF16)

    groups = ((0, 1, 2), (3, 4))

    def copy_x(g, way):
        rows = slice(groups[g][0], groups[g][-1] + 1)
        side = 0 if way == 1 else 2
        return remote(
            sq.at[1, rows], sq.at[side, rows], sem_x, (0 if way == 1 else 1, g), (way, 0, 0)
        )

    for x in range(10):
        v = nt(tap[x // 5], w_in[x - 3 * (x // 5)])
        h1[x] = silu(v + bias[0:1, 0:256]).astype(BF16).reshape(9, 2, 16, 256)
    for g, group in enumerate(groups):
        for x in range(2 * group[0], 2 * group[-1] + 2):
            v = nn(h1[x].reshape(288, 256), w_pf[...]) + bias[0:1, 256:384]
            v = silu(v).astype(BF16).reshape(9, 2, 16, 128)
            d1[x, :, :, 0:128] = v[:, 0]
            d1[x, :, :, 128:256] = v[:, 1]
        n = 144 * len(group)
        rows = slice(group[0], group[-1] + 1)
        parts = [
            jnp.concatenate([d1[2 * i + a].reshape(144, 256) for i in group], axis=0)
            for a in (0, 1)
        ]
        v = silu(nt(jnp.concatenate(parts, axis=1), w_pm[...]) + bias[0:1, 384:640]).astype(BF16)
        d2[rows] = v.reshape(len(group), 9, 16, 256)
        v = nt(v, w_squeeze[...]).astype(BF16)
        sq[1, rows] = v.reshape(len(group), 9, 16, 128)
        copy_x(g, 1).start()
        copy_x(g, -1).start()

    for i in range(5):
        if i in (0, 3):
            copy_x(i // 3, 1).wait_recv()
            copy_x(i // 3, -1).wait_recv()
        v = jnp.concatenate([sq[t, i].reshape(144, 128) for t in range(3)], axis=1)
        v = nt(v, w_ac[...]).reshape(9, 16, 256) + d2[i].astype(F32)
        v = v * mask[i]
        mx[i + 1, 1:10] = v.astype(BF16)
        mx[i + 1, 0] = pltpu.roll(v[8], 1, 0).astype(BF16)
        mx[i + 1, 10] = pltpu.roll(v[0], 15, 0).astype(BF16)
        if i == 0:
            mx[6] = roll_rows(mx[1], 12)
        if i == 4:
            mx[0] = roll_rows(mx[5], 4)

    total = None
    for lift in range(3):
        v = jnp.concatenate(
            [mx[lift : lift + 5, step : step + 9].reshape(720, 256) for step in range(3)], axis=1
        )
        term = nt(v, w_middle[lift])
        total = term if total is None else total + term
    c3[...] = silu(total).astype(BF16).reshape(5, 9, 16, 256)

    v = nt(c3[...].reshape(720, 256), rise_mid[...].reshape(512, 256)).reshape(5, 9, 16, 512)
    for x in (0, 9, 1, 2, 3, 4, 5, 6, 7, 8):
        u = v[x // 2, :, :, x % 2 * 256 : x % 2 * 256 + 256] + d1[x].astype(F32)
        u = u * mask2[x]
        v2[x + 1, 1:10] = u.astype(BF16)
        v2[x + 1, 0, :, 128:256] = pltpu.roll(u[8, :, 128:256], 1, 0).astype(BF16)
        v2[x + 1, 10, :, 0:128] = pltpu.roll(u[0, :, 0:128], 15, 0).astype(BF16)
        if x == 0:
            v2[11] = roll_rows(v2[1], 12)
        if x == 9:
            v2[0] = roll_rows(v2[10], 4)

    weight = rise_fine[...].reshape(256, 128)
    for i in (0, 4, 1, 2, 3):
        parts = []
        for lift in range(3):
            rows = slice(2 * i + lift, 2 * i + lift + 2)
            parts.append(v2[rows, 1:10].reshape(288, 256))
            parts.append(v2[rows, 2:11, :, 0:128].reshape(288, 128))
            parts.append(v2[rows, 0:9, :, 128:256].reshape(288, 128))
        v = silu(nt(jnp.concatenate(parts, axis=1), w_dm[...])).astype(BF16)
        e2[2 * i : 2 * i + 2] = v.reshape(2, 9, 16, 256)
    for i in (0, 4, 1, 2, 3):
        for b in (0, 1):
            v = e2[2 * i : 2 * i + 2, :, :, b * 128 : b * 128 + 128].reshape(288, 128)
            u = nt(v, weight).reshape(2, 9, 16, 256)
            u = u + h1[2 * i : 2 * i + 2, :, b].astype(F32)
            put_phases(f1m, f1s, 2 * i, b, u * mask2[2 * i : 2 * i + 2])
        if i == 0:
            close_below(f1m, f1s)
        if i == 4:
            close_above(f1m, f1s)

    for x in (0, 9, 1, 2, 3, 4, 5, 6, 7, 8):
        v = silu(nt(phase_window(f1m, f1s, x, 1), w_df[...])).reshape(1, 9, 2, 16, 256)
        for b in (0, 1):
            put_phases(f2m, f2s, x, b, v[:, :, b] * mask2[x : x + 1])
        if x == 0:
            close_below(f2m, f2s)
        if x == 9:
            close_above(f2m, f2s)

    parts = []
    for x in range(12):
        for low in (0, 128):
            if (x, low) not in ((0, 0), (11, 128)):
                parts.append(f2m[x, :, :, :, low : low + 128].reshape(288, 128))
                parts.append(f2s[x, 1:10, :, :, low : low + 128].reshape(288, 128))
    out = nt(jnp.concatenate(parts, axis=1), w_lv[...])

    turned[...] = out.T.reshape(16, 2, 8, 288)
    total = None
    for b in (0, 1):
        line = iota((288, 512), 0)
        lane = iota((288, 512), 1)
        block = lax.rem(line, 16)
        tgt = 36 * lax.rem(block, 4) + 2 * (line // 16) + b - 8
        spot = onehot((block // 4 == lane // 128) & (tgt == lax.rem(lane, 128)))
        term = nn(turned[0:10, b].reshape(80, 288).astype(BF16), spot)
        total = term if total is None else total + term
    for rb in range(4):
        outf[rb] = total[:, rb * 128 : rb * 128 + 128]
    for rb in range(4):
        begin, end = max(0, 4 - 10 * rb), min(10, 36 - 10 * rb)
        for a in (0, 1):
            for o in range(3):
                guess[o, pl.ds(20 * rb + 2 * begin + a - 8, end - begin, stride=2), :] = outf[
                    rb, pl.ds(8 * begin + 3 * a + o, end - begin, stride=8), :
                ]
    for c in range(3):
        clean = (noisy[0, c].astype(F32) - coef[0, 0:1] * guess[c]) / coef[1, 0:1]
        kept[c] = coef[2, 0:1] * clean

    for jj in pieces:
        copy_c(jj).wait_send()
    for copy in (below, above, after, before):
        copy.wait_send()
    for j, k in rest:
        copy_h(j, k).wait_send()
    for k in far:
        copy_s(k).wait_send()
    for g in range(2):
        copy_x(g, 1).wait_send()
        copy_x(g, -1).wait_send()


def solution(mesh):
    sizes = tuple(mesh.shape[a] for a in ("plane", "span", "height"))
    planes, spans, heights = sizes

    def shards(*args):
        args = list(args)
        args[5] = args[5].T
        args[6] = args[6].transpose(0, 2, 1)
        args[7] = args[7].transpose(0, 2, 1)
        in_vmem = pl.BlockSpec(memory_space=pltpu.VMEM)
        in_smem = pl.BlockSpec(memory_space=pltpu.SMEM)
        in_any = pl.BlockSpec(memory_space=pl.ANY)
        vmem = pltpu.VMEM
        order = [1, 0] + list(range(4, 17))
        scratch = [vmem(args[k].shape, args[k].dtype) for k in order] + [
            vmem((2, planes // 2, 3, 32, 256), BF16),
            vmem((planes // 2, 3, 32, 256), BF16),
            vmem((planes // 2, 3, 40, 256), F32),
            vmem((48, 256), F32),
            vmem((planes // 2, heights, 5, 8, 256), BF16),
            vmem((planes // 2, heights, 5, 8, 256), BF16),
            vmem((5, 8, 256), F32),
            vmem((spans, 8, 128), BF16),
            vmem((spans, 8, 128), BF16),
            vmem((3, 3, 96, 128), BF16),
            vmem((2, 96, 128), F32),
            vmem((8, 256, 128), F32),
            vmem((2, 288, 512), F32),
            vmem((2, 288, 512), BF16),
            vmem((160, 128), F32),
            vmem((8, 640), F32),
            vmem((3, 8, 128), F32),
            vmem((256, 512), F32),
            vmem((7, 256, 512), BF16),
            vmem((256, 128), BF16),
            vmem((256, 512), BF16),
            vmem((256, 384), BF16),
            vmem((256, 1536), BF16),
            vmem((256, 1024), BF16),
            vmem((16, 1024), F32),
            vmem((256, 5632), BF16),
            vmem((5, 9, 16, 256), F32),
            vmem((10, 9, 16, 256), F32),
            vmem((10, 9, 2, 16, 256), BF16),
            vmem((10, 9, 16, 256), BF16),
            vmem((5, 9, 16, 256), BF16),
            vmem((3, 5, 9, 16, 128), BF16),
            vmem((7, 11, 16, 256), BF16),
            vmem((5, 9, 16, 256), BF16),
            vmem((12, 11, 16, 256), BF16),
            vmem((10, 9, 16, 256), BF16),
            vmem((12, 9, 2, 16, 256), BF16),
            vmem((12, 11, 2, 16, 256), BF16),
            vmem((12, 9, 2, 16, 256), BF16),
            vmem((12, 11, 2, 16, 256), BF16),
            vmem((16, 2, 8, 288), F32),
            vmem((4, 80, 128), F32),
            pltpu.SemaphoreType.DMA((15,)),
            pltpu.SemaphoreType.DMA((2, planes // 2)),
            pltpu.SemaphoreType.DMA((2, planes // 2, heights)),
            pltpu.SemaphoreType.DMA((2, spans)),
            pltpu.SemaphoreType.DMA((2, 4)),
            pltpu.SemaphoreType.DMA((2, 2, 2)),
        ]
        guess, kept, again = pl.pallas_call(
            lambda *refs: body(sizes, *refs),
            out_shape=(
                jax.ShapeDtypeStruct((3, 64, 128), F32),
                jax.ShapeDtypeStruct((3, 64, 128), F32),
                jax.ShapeDtypeStruct((64, 128), F32),
            ),
            in_specs=[in_any, in_any, in_smem, in_smem] + [in_any] * 13,
            out_specs=(in_vmem, in_vmem, in_vmem),
            scratch_shapes=scratch,
            compiler_params=pltpu.CompilerParams(
                collective_id=0, has_side_effects=True, vmem_limit_bytes=56 * 1024 * 1024
            ),
            name="denoise",
        )(*args)
        return guess[None].astype(BF16), (kept + again * guess)[None]

    in_specs = (
        P("plane", None, "height", "span"),
        P(("plane", "span", "height"), None, None, None, None),
    ) + (P(),) * 15
    out_specs = (P("plane", None, "height", "span"), P("plane", None, "height", "span"))
    return jax.shard_map(shards, mesh=mesh, in_specs=in_specs, out_specs=out_specs, check_vma=False)
```

```python
import math

import jax
import jax.numpy as jnp
from jax import lax
from jax.experimental import pallas as pl
from jax.experimental.pallas import tpu as pltpu
from jax.sharding import PartitionSpec as P

TSTEPS = 1000
STRIDE = 20
F32 = jnp.float32
BF16 = jnp.bfloat16
MESH = pl.DeviceIdType.MESH
HIGHEST = lax.Precision.HIGHEST


def nt(a, b):
    return lax.dot_general(a, b, (((1,), (1,)), ((), ())), preferred_element_type=F32)


def nn(a, b):
    return lax.dot_general(a, b, (((1,), (0,)), ((), ())), preferred_element_type=F32)


def tn(a, b):
    return lax.dot_general(a, b, (((0,), (0,)), ((), ())), preferred_element_type=F32)


def silu(v):
    return v * (0.5 * jnp.tanh(0.5 * v) + 0.5)


def iota(shape, dim):
    return lax.broadcasted_iota(jnp.int32, shape, dim)


def onehot(cond):
    return jnp.where(cond, 1.0, 0.0).astype(BF16)


def roll_rows(v, shift):
    return pltpu.roll(v.astype(F32), shift, v.ndim - 2).astype(BF16)


def plan_of(step):
    phase = (step / TSTEPS + 0.008) / 1.008 * (math.pi / 2.0)
    return jnp.cos(phase) ** 2


WINDOW = ((0, 128), (256, 512), (384, 640), (768, 896))


def phase_window(main, side, x, n):
    def flat(v):
        return v.reshape(n * 288, v.shape[-1])

    above, here, below = slice(x, x + n), slice(x + 1, x + 1 + n), slice(x + 2, x + 2 + n)
    return jnp.concatenate(
        [
            flat(main[above, :, :, :, 128:256]),
            flat(side[above, 1:10, :, :, 128:256]),
            flat(main[here]),
            flat(side[here, 1:10]),
            flat(main[below, :, :, :, 0:128]),
            flat(side[below, 1:10, :, :, 0:128]),
        ],
        axis=1,
    )


def put_phases(main, side, x, b, v):
    rows = slice(x + 1, x + 1 + v.shape[0])
    below, above = (slice(1, 10), slice(2, 11)) if b else (slice(0, 9), slice(1, 10))
    edge = pltpu.roll(v[:, 8], 1, 1) if b else pltpu.roll(v[:, 0], 15, 1)
    v, edge = v.astype(BF16), edge.astype(BF16)
    main[rows, :, b] = v
    for low in (0, 128):
        side[rows, below, 1 - b, :, low : low + 64] = v[..., low : low + 64]
        side[rows, above, 1 - b, :, low + 64 : low + 128] = v[..., low + 64 : low + 128]
    for low in (0, 128):
        if b:
            side[rows, 1, 0, :, low + 64 : low + 128] = edge[..., low + 64 : low + 128]
        else:
            side[rows, 9, 1, :, low : low + 64] = edge[..., low : low + 64]


def close_below(main, side):
    main[11, :, :, :, 0:128] = roll_rows(main[1, :, :, :, 0:128], 12)
    side[11, 1:10, :, :, 0:128] = roll_rows(side[1, 1:10, :, :, 0:128], 12)


def close_above(main, side):
    main[0, :, :, :, 128:256] = roll_rows(main[10, :, :, :, 128:256], 4)
    side[0, 1:10, :, :, 128:256] = roll_rows(side[10, 1:10, :, :, 128:256], 4)


def body(sizes, noisy_hbm, slot_hbm, timestep, owner, *refs):
    weights_hbm, outputs, local, refs = refs[:13], refs[13:16], refs[16:31], refs[31:]
    guess, kept, again = outputs
    slot, noisy, *weights = local
    (w_embed, w_biases, w_enter, pool_fine, pool_mid, w_squeeze, w_across) = weights[:7]
    (w_middle, rise_mid, decode_mid, rise_fine, decode_fine, w_leave) = weights[7:]
    (send_p, got_c, planef, heightf, send_h, got_h, rowsf, send_s, got_s) = refs[:9]
    (pick_in, pick_cell, pick_out) = refs[9:12]
    refs = refs[12:]
    (around, aroundf, entryf, tapf, tap, condf, bias, coef, bandf, w_in, w_pf, w_pm) = refs[:12]
    (w_ac, w_dm, w_df, leavef, w_lv, mask, mask2, h1, d1, d2, sq, mx, c3, v2, e2) = refs[12:27]
    (f1m, f1s, f2m, f2s, turned, outf) = refs[27:33]
    (sem_w, sem_c, sem_h, sem_s, sem_n, sem_x) = refs[33:]
    planes, spans, heights = sizes
    p, s, h = (lax.axis_index(a) for a in ("plane", "span", "height"))

    def at(dp, ds, dh):
        return (
            lax.rem(p + (dp + planes), planes),
            lax.rem(s + (ds + spans), spans),
            lax.rem(h + (dh + heights), heights),
        )

    core = lax.rem(p, 2)
    mate = 1 - 2 * core
    chip = p // 2
    chips = planes // 2

    loads = [
        pltpu.make_async_copy(src, dst, sem_w.at[k])
        for k, (src, dst) in enumerate(zip((slot_hbm, noisy_hbm) + weights_hbm, local))
    ]
    for load in loads:
        load.start()

    barrier = pltpu.get_barrier_semaphore()
    partners = [(mate, 0, 0), (-mate, 0, 0)]
    partners += [(2 * j, 0, k) for j in range(chips) for k in range(heights) if j or k]
    partners += [(0, k, 0) for k in range(1, spans)]
    for offset in partners:
        pl.semaphore_signal(barrier, inc=1, device_id=at(*offset), device_id_type=MESH)
    def remote(src, dst, sems, index, offset):
        return pltpu.make_async_remote_copy(
            src_ref=src,
            dst_ref=dst,
            send_sem=sems.at[(0,) + index],
            recv_sem=sems.at[(1,) + index],
            device_id=at(*offset),
            device_id_type=MESH,
        )

    loads[0].wait()
    loads[1].wait()
    mine = (owner[0] == (p * spans + s) * heights + h).astype(F32)
    for k in range(planes):
        send_p[k % 2, k // 2] = (slot[0, k].astype(F32) * mine).astype(BF16)
    pl.semaphore_wait(barrier, len(partners))
    pieces = [jj for jj in (2, 1, 3, 0) if jj < chips]

    def copy_c(jj):
        src = send_p.at[1 - core, lax.rem(chip + jj, chips)]
        return remote(src, got_c.at[jj], sem_c, (jj,), (mate, 0, 0))

    for jj in pieces:
        copy_c(jj).start()

    below = remote(
        noisy.at[0, :, 48:64], around.at[1, :, 0:16], sem_n, (0,), (0, 0, 1)
    )
    above = remote(
        noisy.at[0, :, 0:16], around.at[1, :, 80:96], sem_n, (1,), (0, 0, -1)
    )
    after = remote(around.at[1], around.at[0], sem_n, (2,), (0, 1, 0))
    before = remote(around.at[1], around.at[2], sem_n, (3,), (0, -1, 0))
    below.start()
    above.start()
    around[1, :, 16:80, :] = noisy[0]

    heightf[...] = jnp.zeros_like(heightf)
    planef[...] = jnp.zeros_like(planef)

    def copy_h(jj, k):
        src = send_h.at[jj, lax.rem(h + k, heights)]
        return remote(src, got_h.at[chip, h], sem_h, (jj, k), (2 * jj, 0, k))

    rest = [(jj, k) for jj in pieces for k in (2, 1, 3, 0) if k < heights and (jj or k)]
    for jj in pieces:
        copy_c(jj).wait_recv()
        sent = send_p[core, lax.rem(chip + jj, chips)].astype(F32)
        planef[jj, :, 2:34, :] = sent + got_c[jj].astype(F32)
        for k in range(heights):
            for c in range(3):
                heightf[12 * c : 12 * c + 12, :] = planef[jj, c, 8 * k : 8 * k + 12, :]
            send_h[jj, k] = heightf[0:40, :].reshape(5, 8, 256).astype(BF16)
        for k in (2, 1, 3, 0):
            if k < heights and (jj or k):
                copy_h(jj, k).start()
    got_h[chip, h] = send_h[0, h]
    below.wait_recv()
    above.wait_recv()
    after.start()
    before.start()
    for load in loads[2:]:
        load.wait()

    now_step = jnp.full((8, 128), timestep[0].astype(F32), F32)
    now = plan_of(now_step)
    prior = plan_of(now_step - STRIDE)
    coef[0] = jnp.sqrt(1.0 - now)
    coef[1] = jnp.sqrt(now)
    coef[2] = jnp.sqrt(prior)
    again[...] = jnp.broadcast_to(jnp.sqrt(1.0 - prior)[0:1], (64, 128))
    lane = iota((8, 64), 1)
    order = jnp.where(lane < 32, lane, lane - 32).astype(F32)
    angle = timestep[0].astype(F32) * jnp.exp(order * (-math.log(10000.0) / 32))
    waves = jnp.where(lane < 32, jnp.sin(angle), jnp.cos(angle))
    hidden = jnp.dot(waves, w_embed[...], precision=HIGHEST, preferred_element_type=F32)
    hidden = hidden / (1.0 + jnp.exp(-hidden))
    flat = lax.dot_general(
        hidden, w_biases[...], (((1,), (1,)), ((), ())), HIGHEST, preferred_element_type=F32
    )
    col = iota((448, 640), 1)
    pick = jnp.where(col < 256, lax.rem(col, 64), col - 192)
    pick = jnp.where(iota((448, 640), 0) == pick, 1.0, 0.0)
    bias[...] = jnp.dot(flat, pick, precision=HIGHEST, preferred_element_type=F32)

    w_df[...] = jnp.zeros_like(w_df)
    w_lv[...] = jnp.zeros_like(w_lv)
    leavef[...] = jnp.zeros_like(leavef)
    for b in (0, 1):
        place = iota((192, 256), 1)
        tapcol = lax.rem(place // 64 + 1, 4) - b
        spot = onehot(
            (tapcol >= 0)
            & (tapcol <= 2)
            & (iota((192, 256), 0) == tapcol * 64 + lax.rem(place, 64))
        )
        for lift in range(3):
            block = nn(decode_fine[lift], spot).astype(BF16)
            final = nn(w_leave[lift], spot)
            for a in (0, 1):
                first, second = WINDOW[a + lift]
                rows = slice(a * 128 + b * 64, a * 128 + b * 64 + 64)
                w_df[rows, first : first + 128] = block[:, 0:128]
                w_df[rows, second : second + 128] = block[:, 128:256]
                rows = slice(b * 8 + a * 3, b * 8 + a * 3 + 3)
                leavef[rows, first : first + 128] = final[:, 0:128]
                leavef[rows, second : second + 128] = final[:, 128:256]
    final = leavef[...].astype(BF16)
    for x in range(10):
        for k, begin in enumerate((0, 128, 256, 512, 384, 640, 768, 896)):
            spot = 512 * x + 128 * k
            w_lv[16 * x : 16 * x + 16, spot : spot + 128] = final[:, begin : begin + 128]

    for k in range(4):
        w_pf[k * 64 : k * 64 + 64, :] = pool_fine[k]
        w_pm[:, k * 128 : k * 128 + 128] = pool_mid[k]
    has_before = (p > 0).astype(F32)
    has_after = (p < planes - 1).astype(F32)
    w_ac[:, 0:128] = (w_across[0].astype(F32) * has_before).astype(BF16)
    w_ac[:, 128:256] = w_across[1]
    w_ac[:, 256:384] = (w_across[2].astype(F32) * has_after).astype(BF16)
    w_dm[...] = jnp.zeros_like(w_dm)
    for b in (0, 1):
        for lift in range(3):
            for step in range(3):
                spot = 512 * lift + 128 * ((b + step + 3) % 4)
                w_dm[b * 128 : b * 128 + 128, spot : spot + 128] = decode_mid[
                    lift, :, step * 128 : step * 128 + 128
                ]

    for a in (0, 1):
        for b in (0, 1):
            total = None
            for lift in range(3):
                k = iota((18, 512), 0)
                tgt = (k // 6 + b) * 128 + (a + lift) * 8 + lax.rem(k, 6)
                term = tn(w_enter[lift], onehot(iota((18, 512), 1) == tgt))
                total = term if total is None else total + term
            bandf[a * 128 + b * 64 : a * 128 + b * 64 + 64, :] = total
    for x in range(7):
        for wc in range(4):
            lanes = slice(wc * 128, wc * 128 + 128)
            v = bandf[:, lanes]
            w_in[x, :, lanes] = (v if x == 0 else pltpu.roll(v, 16 * x, 1)).astype(BF16)

    shape = (5, 9, 16, 256)
    block = iota(shape, 2)
    row = (block // 4) * 5 + iota(shape, 0) - 2
    col = lax.rem(block, 4) * 9 + iota(shape, 1) - 2
    low_row, high_row = jnp.where(h == 0, 0, -9), jnp.where(h == heights - 1, 16, 99)
    low_col, high_col = jnp.where(s == 0, 0, -9), jnp.where(s == spans - 1, 32, 99)
    inside = (row >= low_row) & (row < high_row) & (col >= low_col) & (col < high_col)
    mask[...] = jnp.where(inside, 1.0, 0.0)
    for x in range(10):
        mask2[x] = mask[x // 2]

    after.wait_recv()
    before.wait_recv()
    row = iota((96, 128), 0)
    rows_in = jnp.where((row >= jnp.where(h == 0, 16, 0)) & (row < jnp.where(h == heights - 1, 80, 96)), 1.0, 0.0)
    right = rows_in * (s < spans - 1).astype(F32)
    left = rows_in * (s > 0).astype(F32)
    near = iota((96, 128), 1) < 64
    entryf[...] = jnp.zeros_like(entryf)
    for c in range(3):
        aroundf[0] = around[1, c].astype(F32) * rows_in
        aroundf[1] = jnp.where(
            near, around[2, c].astype(F32) * right, around[0, c].astype(F32) * left
        )
        for rb in range(4):
            for part in range(2):
                entryf[2 * rb + part, pl.ds(c, 22, stride=8), :] = aroundf[
                    part, 7 + 20 * rb : 29 + 20 * rb, :
                ]
    entry = jnp.concatenate([entryf[k] for k in range(8)], axis=1).astype(BF16)
    line = iota((288, 1), 0)
    block = lax.rem(line, 16)
    cell = 36 * lax.rem(block, 4) + 2 * (line // 16) - 9
    for wc in range(4):
        tgt = (block // 4) * 256 + ((cell + wc) & 255)
        spot = onehot(iota((288, 1024), 1) == tgt)
        for g in range(2):
            tapf[g, :, wc * 128 : wc * 128 + 128] = nt(spot, entry[48 * g : 48 * g + 128])

    for j, k in rest:
        copy_h(j, k).wait_recv()
    total = None
    for j in range(chips):
        for k in range(heights):
            term = got_h[j, k].astype(F32)
            total = term if total is None else total + term
    rowsf[...] = total

    moved = [rowsf[0]] + [pltpu.roll(rowsf[g], 24 * g, 1) for g in range(1, 5)]
    for dest in range(spans):
        rel = (iota((8, 256), 1) - (16 * dest - 2)) & 255
        total = moved[0]
        for g in range(1, 5):
            total = jnp.where(rel >= 24 * g, moved[g], total)
        total = pltpu.roll(total, (2 - 16 * dest) % 256, 1)[:, 0:128]
        send_s[dest] = total.astype(BF16)

    def copy_s(k):
        return remote(send_s.at[lax.rem(s + k, spans)], got_s.at[s], sem_s, (k,), (0, k, 0))

    far = sorted(range(1, spans), key=lambda k: -min(k, spans - k))
    for k in far:
        copy_s(k).start()
    got_s[s] = send_s[s]
    line = iota((256, 160), 0)
    channel = lax.rem(line, 8) - 3
    m = iota((256, 160), 1)
    rb = m // 40
    tgt = channel * 12 + (rb * 20 + line // 8 + 7) // 8
    pick = (channel >= 0) & (channel < 3) & (line < 176) & (m - 40 * rb == tgt)
    pick_in[...] = onehot(pick)
    line = iota((288, 1), 0)
    block = lax.rem(line, 16)
    cell = 36 * lax.rem(block, 4) + 2 * (line // 16) - 9
    for wc in range(4):
        tgt = (block // 4) * 32 + (cell + wc + 16) // 8
        pick_cell[wc] = onehot(iota((288, 128), 1) == tgt)
    lane = iota((1, 512), 1)
    for b in (0, 1):
        col = cell + 1 + b
        tgt = jnp.where((col >= 0) & (col < 128), (block // 4) * 128 + col, -1)
        pick_out[b] = onehot(lane == tgt)
    for k in reversed(far):
        copy_s(k).wait_recv()
    total = got_s[0].astype(F32)
    for k in range(1, spans):
        total = total + got_s[k].astype(F32)
    lane = iota((8, 128), 1)
    spot = lane - 24 * (lane // 24)
    outside = ((spot < 2) & (s == 0)) | ((spot >= 18) & (s == spans - 1))
    total = jnp.where(outside, 0.0, total)
    for g in range(5):
        part = total if g == 0 else pltpu.roll(total, 128 - 24 * g, 1)
        part = jnp.where(lane < 20, part, 0.0)
        for rb in range(4):
            condf[rb * 40 + 8 * g : rb * 40 + 8 * g + 8, :] = (
                part if rb == 0 else pltpu.roll(part, 32 * rb, 1)
            )
    lifted = nn(pick_in[...], condf[...].astype(BF16)).astype(BF16)
    for wc in range(4):
        lanes = slice(wc * 128, wc * 128 + 128)
        for g in range(2):
            v = tapf[g, :, lanes] + nt(pick_cell[wc], lifted[48 * g : 48 * g + 128])
            tap[g, :, lanes] = v.astype(BF16)

    groups = ((0, 1, 2), (3, 4))

    def copy_x(g, way):
        rows = slice(groups[g][0], groups[g][-1] + 1)
        side = 0 if way == 1 else 2
        return remote(
            sq.at[1, rows], sq.at[side, rows], sem_x, (0 if way == 1 else 1, g), (way, 0, 0)
        )

    for x in range(10):
        v = nt(tap[x // 5], w_in[x - 3 * (x // 5)])
        h1[x] = silu(v + bias[0:1, 0:256]).astype(BF16).reshape(9, 2, 16, 256)
    for g, group in enumerate(groups):
        for x in range(2 * group[0], 2 * group[-1] + 2):
            v = nn(h1[x].reshape(288, 256), w_pf[...]) + bias[0:1, 256:384]
            v = silu(v).astype(BF16).reshape(9, 2, 16, 128)
            d1[x, :, :, 0:128] = v[:, 0]
            d1[x, :, :, 128:256] = v[:, 1]
        n = 144 * len(group)
        rows = slice(group[0], group[-1] + 1)
        parts = [
            jnp.concatenate([d1[2 * i + a].reshape(144, 256) for i in group], axis=0)
            for a in (0, 1)
        ]
        v = silu(nt(jnp.concatenate(parts, axis=1), w_pm[...]) + bias[0:1, 384:640]).astype(BF16)
        d2[rows] = v.reshape(len(group), 9, 16, 256)
        v = nt(v, w_squeeze[...]).astype(BF16)
        sq[1, rows] = v.reshape(len(group), 9, 16, 128)
        copy_x(g, 1).start()
        copy_x(g, -1).start()

    for i in range(5):
        if i in (0, 3):
            copy_x(i // 3, 1).wait_recv()
            copy_x(i // 3, -1).wait_recv()
        v = jnp.concatenate([sq[t, i].reshape(144, 128) for t in range(3)], axis=1)
        v = nt(v, w_ac[...]).reshape(9, 16, 256) + d2[i].astype(F32)
        v = v * mask[i]
        mx[i + 1, 1:10] = v.astype(BF16)
        mx[i + 1, 0] = pltpu.roll(v[8], 1, 0).astype(BF16)
        mx[i + 1, 10] = pltpu.roll(v[0], 15, 0).astype(BF16)
        if i == 0:
            mx[6] = roll_rows(mx[1], 12)
        if i == 4:
            mx[0] = roll_rows(mx[5], 4)

    total = None
    for lift in range(3):
        v = jnp.concatenate(
            [mx[lift : lift + 5, step : step + 9].reshape(720, 256) for step in range(3)], axis=1
        )
        term = nt(v, w_middle[lift])
        total = term if total is None else total + term
    c3[...] = silu(total).astype(BF16).reshape(5, 9, 16, 256)

    v = nt(c3[...].reshape(720, 256), rise_mid[...].reshape(512, 256)).reshape(5, 9, 16, 512)
    for x in (0, 9, 1, 2, 3, 4, 5, 6, 7, 8):
        u = v[x // 2, :, :, x % 2 * 256 : x % 2 * 256 + 256] + d1[x].astype(F32)
        u = u * mask2[x]
        v2[x + 1, 1:10] = u.astype(BF16)
        v2[x + 1, 0, :, 128:256] = pltpu.roll(u[8, :, 128:256], 1, 0).astype(BF16)
        v2[x + 1, 10, :, 0:128] = pltpu.roll(u[0, :, 0:128], 15, 0).astype(BF16)
        if x == 0:
            v2[11] = roll_rows(v2[1], 12)
        if x == 9:
            v2[0] = roll_rows(v2[10], 4)

    weight = rise_fine[...].reshape(256, 128)
    for i in (0, 4, 1, 2, 3):
        parts = []
        for lift in range(3):
            rows = slice(2 * i + lift, 2 * i + lift + 2)
            parts.append(v2[rows, 1:10].reshape(288, 256))
            parts.append(v2[rows, 2:11, :, 0:128].reshape(288, 128))
            parts.append(v2[rows, 0:9, :, 128:256].reshape(288, 128))
        v = silu(nt(jnp.concatenate(parts, axis=1), w_dm[...])).astype(BF16)
        e2[2 * i : 2 * i + 2] = v.reshape(2, 9, 16, 256)
    for i in (0, 4, 1, 2, 3):
        for b in (0, 1):
            v = e2[2 * i : 2 * i + 2, :, :, b * 128 : b * 128 + 128].reshape(288, 128)
            u = nt(v, weight).reshape(2, 9, 16, 256)
            u = u + h1[2 * i : 2 * i + 2, :, b].astype(F32)
            put_phases(f1m, f1s, 2 * i, b, u * mask2[2 * i : 2 * i + 2])
        if i == 0:
            close_below(f1m, f1s)
        if i == 4:
            close_above(f1m, f1s)

    for x in (0, 9, 1, 2, 3, 4, 5, 6, 7, 8):
        v = silu(nt(phase_window(f1m, f1s, x, 1), w_df[...])).reshape(1, 9, 2, 16, 256)
        for b in (0, 1):
            put_phases(f2m, f2s, x, b, v[:, :, b] * mask2[x : x + 1])
        if x == 0:
            close_below(f2m, f2s)
        if x == 9:
            close_above(f2m, f2s)

    parts = []
    for x in range(12):
        for low in (0, 128):
            if (x, low) not in ((0, 0), (11, 128)):
                parts.append(f2m[x, :, :, :, low : low + 128].reshape(288, 128))
                parts.append(f2s[x, 1:10, :, :, low : low + 128].reshape(288, 128))
    out = nt(jnp.concatenate(parts, axis=1), w_lv[...])

    turned[...] = out.T.reshape(16, 2, 8, 288)
    total = None
    for b in (0, 1):
        term = nn(turned[0:10, b].reshape(80, 288).astype(BF16), pick_out[b])
        total = term if total is None else total + term
    for rb in range(4):
        outf[rb] = total[:, rb * 128 : rb * 128 + 128]
    for rb in range(4):
        begin, end = max(0, 4 - 10 * rb), min(10, 36 - 10 * rb)
        for a in (0, 1):
            for o in range(3):
                guess[o, pl.ds(20 * rb + 2 * begin + a - 8, end - begin, stride=2), :] = outf[
                    rb, pl.ds(8 * begin + 3 * a + o, end - begin, stride=8), :
                ]
    for c in range(3):
        clean = (noisy[0, c].astype(F32) - coef[0, 0:1] * guess[c]) / coef[1, 0:1]
        kept[c] = coef[2, 0:1] * clean

    for jj in pieces:
        copy_c(jj).wait_send()
    for copy in (below, above, after, before):
        copy.wait_send()
    for j, k in rest:
        copy_h(j, k).wait_send()
    for k in far:
        copy_s(k).wait_send()
    for g in range(2):
        copy_x(g, 1).wait_send()
        copy_x(g, -1).wait_send()


def solution(mesh):
    sizes = tuple(mesh.shape[a] for a in ("plane", "span", "height"))
    planes, spans, heights = sizes

    def shards(*args):
        args = list(args)
        args[5] = args[5].T
        args[6] = args[6].transpose(0, 2, 1)
        args[7] = args[7].transpose(0, 2, 1)
        in_vmem = pl.BlockSpec(memory_space=pltpu.VMEM)
        in_smem = pl.BlockSpec(memory_space=pltpu.SMEM)
        in_any = pl.BlockSpec(memory_space=pl.ANY)
        vmem = pltpu.VMEM
        order = [1, 0] + list(range(4, 17))
        scratch = [vmem(args[k].shape, args[k].dtype) for k in order] + [
            vmem((2, planes // 2, 3, 32, 256), BF16),
            vmem((planes // 2, 3, 32, 256), BF16),
            vmem((planes // 2, 3, 40, 256), F32),
            vmem((48, 256), F32),
            vmem((planes // 2, heights, 5, 8, 256), BF16),
            vmem((planes // 2, heights, 5, 8, 256), BF16),
            vmem((5, 8, 256), F32),
            vmem((spans, 8, 128), BF16),
            vmem((spans, 8, 128), BF16),
            vmem((256, 160), BF16),
            vmem((4, 288, 128), BF16),
            vmem((2, 288, 512), BF16),
            vmem((3, 3, 96, 128), BF16),
            vmem((2, 96, 128), F32),
            vmem((8, 256, 128), F32),
            vmem((2, 288, 512), F32),
            vmem((2, 288, 512), BF16),
            vmem((160, 128), F32),
            vmem((8, 640), F32),
            vmem((3, 8, 128), F32),
            vmem((256, 512), F32),
            vmem((7, 256, 512), BF16),
            vmem((256, 128), BF16),
            vmem((256, 512), BF16),
            vmem((256, 384), BF16),
            vmem((256, 1536), BF16),
            vmem((256, 1024), BF16),
            vmem((16, 1024), F32),
            vmem((256, 5632), BF16),
            vmem((5, 9, 16, 256), F32),
            vmem((10, 9, 16, 256), F32),
            vmem((10, 9, 2, 16, 256), BF16),
            vmem((10, 9, 16, 256), BF16),
            vmem((5, 9, 16, 256), BF16),
            vmem((3, 5, 9, 16, 128), BF16),
            vmem((7, 11, 16, 256), BF16),
            vmem((5, 9, 16, 256), BF16),
            vmem((12, 11, 16, 256), BF16),
            vmem((10, 9, 16, 256), BF16),
            vmem((12, 9, 2, 16, 256), BF16),
            vmem((12, 11, 2, 16, 256), BF16),
            vmem((12, 9, 2, 16, 256), BF16),
            vmem((12, 11, 2, 16, 256), BF16),
            vmem((16, 2, 8, 288), F32),
            vmem((4, 80, 128), F32),
            pltpu.SemaphoreType.DMA((15,)),
            pltpu.SemaphoreType.DMA((2, planes // 2)),
            pltpu.SemaphoreType.DMA((2, planes // 2, heights)),
            pltpu.SemaphoreType.DMA((2, spans)),
            pltpu.SemaphoreType.DMA((2, 4)),
            pltpu.SemaphoreType.DMA((2, 2, 2)),
        ]
        guess, kept, again = pl.pallas_call(
            lambda *refs: body(sizes, *refs),
            out_shape=(
                jax.ShapeDtypeStruct((3, 64, 128), F32),
                jax.ShapeDtypeStruct((3, 64, 128), F32),
                jax.ShapeDtypeStruct((64, 128), F32),
            ),
            in_specs=[in_any, in_any, in_smem, in_smem] + [in_any] * 13,
            out_specs=(in_vmem, in_vmem, in_vmem),
            scratch_shapes=scratch,
            compiler_params=pltpu.CompilerParams(
                collective_id=0, has_side_effects=True, vmem_limit_bytes=56 * 1024 * 1024
            ),
            name="denoise",
        )(*args)
        return guess[None].astype(BF16), (kept + again * guess)[None]

    in_specs = (
        P("plane", None, "height", "span"),
        P(("plane", "span", "height"), None, None, None, None),
    ) + (P(),) * 15
    out_specs = (P("plane", None, "height", "span"), P("plane", None, "height", "span"))
    return jax.shard_map(shards, mesh=mesh, in_specs=in_specs, out_specs=out_specs, check_vma=False)
```
